512 devices in a mesh: leaf: 256 (over x, y, z), rep: 2 (over core).
Axes of the slice: x: 4, y: 4, z: 16, core: 2. Of those that a mesh axis runs over, the one named last changes fastest.
Arguments:
- leaf_matrix: bfloat16 [131072, 512], P('leaf')
- leaf_inverse: bfloat16 [131072, 512], P('leaf')
- coupling: bfloat16 [131072, 2048], P('leaf'), may hold values from -0.125 to 0.125
- cubic_coeff: float32 [131072], P('leaf'), may hold values from 0.05 to 0.5
- leaf_load: float32 [131072, 256], P('leaf', 'rep'), may hold values from -6 to 6
- sep_load: float32 [2048, 256], P('leaf', 'rep'), may hold values from -6 to 6
- sep_matrix: float32 [2048, 2048], P(('leaf', 'rep'))
- sep_inverse: float32 [2048, 2048], P(('leaf', 'rep'))
- owner_map: int32 [2048], replicated, may hold values from 0 to 2047, each once
- block_mask: int32 [256, 16], P('leaf'), may hold values 0 or 1
Outputs:
- leaf_solution: float32 [131072, 256], P('leaf', 'rep')
- sep_solution: float32 [2048, 256], P('leaf', 'rep')
The draws below stay inside these ranges and needn't reach their ends.
Inputs may be any that keep to these rules, and one draw needn't show every extreme that they name: `owner_map`: each of the 2048 separator rows appears exactly once.
All inputs are finite; a program needn't handle non-finite values. No bound on the sum of `block_mask` on one device may be relied on, other than what follows from the above.
Results may differ from the reference program's by a relative error of at most 0.0073.
Values sent between devices are 32-bit elements; how exact they have to be, the bound alone decides.
No kernel may reach another device: no remote copies, remote signals or barrier semaphores. Data moves between devices by JAX's collectives and lax.ppermute only.
A program may use at most 64 MiB of HBM per device.

```python
import math
import jax
import jax.numpy as jnp
from jax import lax

B = 512
SG = 2048
STEPS = 2
BLOCK = 128
LEAF_ROWS = 131072
K = 256
NBLK = 16
N_LEAF = 256


def square_pair(key, rows, width, low, high, spread):
    first = jax.random.fold_in(key, 31)
    second = jax.random.fold_in(key, 57)
    diag_vals = jnp.exp(jax.random.uniform(first, (rows,), jnp.float32, jnp.log(low), jnp.log(high)))
    offdiag = jax.random.normal(second, (rows, width), jnp.float32) * (spread / jnp.sqrt(jnp.float32(width)))
    on_diag = jnp.arange(width)[None, :] == (jnp.arange(rows) % width)[:, None]
    col_diag = jnp.repeat(diag_vals.reshape(rows // width, width), width, axis=0)
    matrix = jnp.where(on_diag, diag_vals[:, None], offdiag)
    inverse = jnp.where(on_diag, 1.0 / diag_vals[:, None], -offdiag / (diag_vals[:, None] * col_diag))
    return (matrix, inverse)


def draw_leaf_matrix(key, part):
    return square_pair(jax.random.fold_in(key, 5), LEAF_ROWS, B, 1.0, 4.0, 0.4)[0].astype(jnp.bfloat16)


def draw_leaf_inverse(key, part):
    return square_pair(jax.random.fold_in(key, 5), LEAF_ROWS, B, 1.0, 4.0, 0.4)[1].astype(jnp.bfloat16)


def draw_sep_matrix(key, part):
    return square_pair(jax.random.fold_in(key, 9), SG, SG, 2.0, 6.0, 1.5)[0]


def draw_sep_inverse(key, part):
    return square_pair(jax.random.fold_in(key, 9), SG, SG, 2.0, 6.0, 1.5)[1]


def with_ends(result, key, low, high):
    dims = result.shape
    spot = [jax.random.randint(jax.random.fold_in(key, axis), (), 0, dims[axis]) for axis in range(len(dims))]
    result = result.at[tuple(spot)].set(low)
    longest = dims.index(max(dims))
    spot[longest] = (spot[longest] + 1) % dims[longest]
    return result.at[tuple(spot)].set(high)


def spiked(entries, rng, source, target, shards_of, factor):
    owner, partner = [(jnp.arange(entries.shape[dim]) // (entries.shape[dim] // shards_of)).reshape([-1 if axis == dim else 1 for axis in range(entries.ndim)]) for dim in (source, target)]
    chosen = jax.random.permutation(rng, shards_of)[partner]
    strong = (owner == chosen) | (owner == (partner + shards_of // 2) % shards_of)
    return jnp.where(strong, factor * entries, entries)


def block_levels(stream_key, extent, pieces, least, top_value):
    loudness, own = 1.0, jax.random.fold_in(stream_key, 6)
    for position, shards_of in pieces:
        draws = jnp.exp(jax.random.uniform(jax.random.fold_in(own, position), (shards_of,), jnp.float32, least / len(pieces), top_value / len(pieces)))
        loudness = loudness * jnp.repeat(draws, extent[position] // shards_of).reshape([-1 if axis == position else 1 for axis in range(len(extent))])
    return loudness


def centred(rng, extent, scale, limit, pieces=(), held_as=jnp.bfloat16):
    level = block_levels(rng, extent, pieces, -0.22, 0.18) if pieces else 1.0
    entries = jax.random.normal(rng, extent, jnp.float32) * scale * level
    return jnp.minimum(jnp.maximum(entries, -limit), limit).astype(held_as)


def bell_draw_with(rng, extent, scale, bound, pieces, heavy, dtype=jnp.bfloat16):
    result = scale * jax.random.normal(rng, extent, jnp.float32)
    if pieces:
        result = result * block_levels(rng, extent, pieces, -0.22, 0.18)
    return jnp.clip(spiked(result, jax.random.fold_in(rng, 3), *heavy), -bound, bound).astype(dtype)


def setup_inputs(seed: int = 0) -> dict:
    splits = jax.random.split(jax.random.key(seed), 11)
    leaf_matrix = draw_leaf_matrix(jax.random.fold_in(splits[10], 71), 0)
    leaf_inverse = draw_leaf_inverse(jax.random.fold_in(splits[10], 71), 0)
    coupling = bell_draw_with(splits[2], (LEAF_ROWS, SG), (LEAF_ROWS // 4) ** -0.5, 0.125, ((0, 256),), (0, 1, 256, 6.0))
    cubic_coeff = jnp.clip(jnp.exp(math.log(0.5) - 2.3025851 * jax.random.uniform(splits[3], (LEAF_ROWS,), jnp.float32) ** block_levels(splits[3], (LEAF_ROWS,), ((0, 256),), -0.2, 0.2)), 0.05, 0.5)
    leaf_load = centred(splits[4], (LEAF_ROWS, K), 1.0, 6.0, ((0, 256), (1, 2)), jnp.float32)
    sep_load = centred(splits[5], (SG, K), 1.0, 6.0, ((0, 256), (1, 2)), jnp.float32)
    sep_matrix = draw_sep_matrix(jax.random.fold_in(splits[10], 71), 0)
    sep_inverse = draw_sep_inverse(jax.random.fold_in(splits[10], 71), 0)
    owner_map = jax.random.permutation(splits[8], SG).astype(jnp.int32)
    block_mask = with_ends((jax.random.randint(splits[9], (N_LEAF, NBLK), 0, 4) < 3).astype(jnp.int32), jax.random.fold_in(splits[9], 1), 0, 1)
    return {"leaf_matrix": leaf_matrix, "leaf_inverse": leaf_inverse, "coupling": coupling, "cubic_coeff": cubic_coeff, "leaf_load": leaf_load, "sep_load": sep_load, "sep_matrix": sep_matrix, "sep_inverse": sep_inverse, "owner_map": owner_map, "block_mask": block_mask}


def leaf_columns(block_rows, mask_row, owner_map):
    keep_cols = jnp.repeat(mask_row, BLOCK).astype(jnp.bfloat16)
    return (block_rows * keep_cols[None, :])[:, owner_map]


def wide_dot(left, right):
    return jnp.dot(left.astype(jnp.float32), right.astype(jnp.float32), precision=lax.Precision.HIGHEST, preferred_element_type=jnp.float32)


def reference(leaf_matrix, leaf_inverse, coupling, cubic_coeff, leaf_load, sep_load, sep_matrix, sep_inverse, owner_map, block_mask):
    matrices = leaf_matrix.reshape(N_LEAF, B, B)
    inverses = leaf_inverse.reshape(N_LEAF, B, B)
    couplings = coupling.reshape(N_LEAF, B, SG)
    loads = leaf_load.reshape(N_LEAF, B, K)
    cubics = cubic_coeff.reshape(N_LEAF, B)
    leaf_state = jnp.zeros((N_LEAF, B, K), jnp.float32)
    sep_state = jnp.zeros((SG, K), jnp.float32)
    for newton in range(STEPS):
        def forward(total, items):
            matrix, inverse, block_rows, mask_row, load, cubic, state = items
            columns = leaf_columns(block_rows, mask_row, owner_map)
            resid = load - wide_dot(matrix, state.astype(jnp.bfloat16))
            resid = resid - wide_dot(columns, sep_state.astype(jnp.bfloat16))
            resid = resid - cubic[:, None] * state * state * state
            solved = wide_dot(inverse, resid.astype(jnp.bfloat16))
            mixed = (state + solved).astype(jnp.bfloat16)
            term = wide_dot(columns.T, mixed)
            return total + term, solved

        total, solved_all = lax.scan(forward, jnp.zeros((SG, K), jnp.float32), (matrices, inverses, couplings, block_mask, loads, cubics, leaf_state))
        rhs = sep_load - jnp.dot(sep_matrix, sep_state, precision=lax.Precision.HIGHEST, preferred_element_type=jnp.float32) - total
        delta = jnp.dot(sep_inverse, rhs, precision=lax.Precision.HIGHEST, preferred_element_type=jnp.float32)
        sep_state = sep_state + delta
        delta_half = delta.astype(jnp.bfloat16)

        def backward(carry, items):
            inverse, block_rows, mask_row, solved, state = items
            columns = leaf_columns(block_rows, mask_row, owner_map)
            back = wide_dot(columns, delta_half).astype(jnp.bfloat16)
            return carry, state + solved - wide_dot(inverse, back)

        unused, leaf_state = lax.scan(backward, jnp.zeros((), jnp.float32), (inverses, couplings, block_mask, solved_all, leaf_state))
    return leaf_state.reshape(LEAF_ROWS, K), sep_state
```

```python
import jax
import jax.numpy as jnp
from jax import lax
from jax.experimental import pallas as pl
from jax.experimental.pallas import tpu as pltpu
from jax.sharding import Mesh, PartitionSpec as P

STEPS = 2
BLOCK = 128
NX, NY, NZ, NC = 4, 4, 16, 2
NXY = NX * NY
TILE = 256
F32 = jnp.float32
BF16 = jnp.bfloat16
VMEM_LIMIT = 48 * 1024 * 1024
HIGHEST = lax.Precision.HIGHEST


def dot(left, right):
    return jnp.dot(left, right, preferred_element_type=F32)


def whole(shape):
    return pl.BlockSpec(shape, lambda *_: (0,) * len(shape))


def params():
    return pltpu.CompilerParams(vmem_limit_bytes=VMEM_LIMIT)


def call(kernel, out, *args):
    return pl.pallas_call(kernel, out_shape=out, compiler_params=params())(*args)


def start_kernel(inverse, coupling, load, keep, owner, columns, solved_out, contrib, masked, mixed_t):
    @pl.when(pl.program_id(0) == 0)
    def _():
        masked[...] = coupling[...] * keep[...]
        solved = dot(inverse[...], load[...].astype(BF16))
        solved_out[...] = solved
        mixed_t[...] = solved.T.astype(BF16)

    rows = lax.broadcasted_iota(jnp.int32, (coupling.shape[1], TILE), 0)
    pick = jnp.where(rows == owner[...], 1.0, 0.0).astype(BF16)
    tile = dot(masked[...], pick).astype(BF16)
    columns[...] = tile
    part = dot(mixed_t[...], tile)
    for i in range(TILE // BLOCK):
        contrib[i] = part[:, i * BLOCK : (i + 1) * BLOCK]


def start(inverse, coupling, load, keep, owner):
    width, sep_width = coupling.shape
    cases = load.shape[1]
    return pl.pallas_call(
        start_kernel,
        grid=(sep_width // TILE,),
        in_specs=[
            whole(inverse.shape),
            whole(coupling.shape),
            whole(load.shape),
            whole(keep.shape),
            pl.BlockSpec((1, TILE), lambda j: (0, j)),
        ],
        out_specs=[
            pl.BlockSpec((width, TILE), lambda j: (0, j)),
            whole(load.shape),
            pl.BlockSpec((TILE // BLOCK, cases, BLOCK), lambda j: (j, 0, 0)),
        ],
        out_shape=[
            jax.ShapeDtypeStruct((width, sep_width), BF16),
            jax.ShapeDtypeStruct(load.shape, F32),
            jax.ShapeDtypeStruct((NXY, cases, BLOCK), F32),
        ],
        scratch_shapes=[pltpu.VMEM((width, sep_width), BF16), pltpu.VMEM((cases, width), BF16)],
        compiler_params=params(),
    )(inverse, coupling, load, keep, owner)


def sum_rows_kernel(parts, local_t, out):
    cases = parts.shape[1]
    total = local_t[...] - jnp.sum(parts[...], axis=0)
    out[...] = total.reshape(NZ, cases // NZ, BLOCK)


def sum_cases_kernel(parts, out):
    out[...] = jnp.broadcast_to(jnp.sum(parts[...], axis=0)[None], out.shape)


def delta_kernel(rhs, inverse_rows, out):
    acc = jnp.zeros(rhs.shape[1:], F32)
    for i in range(NXY):
        acc = acc + lax.dot_general(
            rhs[i],
            inverse_rows[:, i * BLOCK : (i + 1) * BLOCK],
            (((1,), (1,)), ((), ())),
            precision=HIGHEST,
            preferred_element_type=F32,
        )
    out[...] = jnp.broadcast_to(acc[None], out.shape)


def spread_kernel(parts, out):
    cases = parts.shape[0] * parts.shape[1]
    out[...] = jnp.broadcast_to(parts[...].reshape(cases, BLOCK).T[None], out.shape)


def middle_kernel(delta, columns, matrix, inverse, load, cubic, solved_in, state_out, contrib):
    coupled = dot(columns[...], delta[...].astype(BF16))
    state = solved_in[...] - dot(inverse[...], coupled.astype(BF16))
    resid = load[...] - dot(matrix[...], state.astype(BF16)) - coupled
    resid = resid - cubic[...] * state * state * state
    mixed = state + dot(inverse[...], resid.astype(BF16))
    state_out[...] = mixed
    part = dot(mixed.T.astype(BF16), columns[...])
    for i in range(NXY):
        contrib[i] = part[:, i * BLOCK : (i + 1) * BLOCK]


def end_kernel(delta, columns, inverse, mixed, out):
    back = dot(columns[...], delta[...].astype(BF16)).astype(BF16)
    out[...] = mixed[...] - dot(inverse[...], back)


def exchange(parts, axes):
    return lax.all_to_all(parts, axes, 0, 0, tiled=True)


def correction(contrib, local, inverse_rows, place):
    cases = contrib.shape[1]
    case_group = cases // NZ
    local_t = lax.dynamic_update_slice_in_dim(jnp.zeros((BLOCK, cases), F32), local, place, 0).T
    parts = exchange(contrib, ("x", "y"))
    parts = call(sum_rows_kernel, jax.ShapeDtypeStruct((NZ, case_group, BLOCK), F32), parts, local_t)
    parts = exchange(parts, "z")
    rhs = call(sum_cases_kernel, jax.ShapeDtypeStruct((NXY, case_group, BLOCK), F32), parts)
    rhs = exchange(rhs, ("x", "y"))
    delta = call(delta_kernel, jax.ShapeDtypeStruct((NZ, case_group, BLOCK), F32), rhs, inverse_rows)
    delta = exchange(delta, "z")
    delta = call(spread_kernel, jax.ShapeDtypeStruct((NXY, BLOCK, cases), F32), delta)
    return exchange(delta, ("x", "y")).reshape(NXY * BLOCK, cases)


def on_device(
    leaf_matrix,
    leaf_inverse,
    coupling,
    cubic_coeff,
    leaf_load,
    sep_load,
    sep_matrix,
    sep_inverse,
    owner_map,
    block_mask,
):
    owned = sep_load.shape[0]
    inverse_rows = lax.all_gather(sep_inverse, ("z", "c"), axis=0, tiled=True)
    matrix_rows = lax.all_gather(sep_matrix, "c", axis=0, tiled=True)
    place = lax.axis_index("z") * owned
    first_row = lax.axis_index(("x", "y", "z")) * owned
    keep = jnp.repeat(block_mask[0], BLOCK).astype(BF16)[None, :]
    columns, solved, contrib = start(leaf_inverse, coupling, leaf_load, keep, owner_map[None, :])

    delta = correction(contrib, sep_load, inverse_rows, place)
    local = sep_load - jnp.dot(matrix_rows, delta, precision=HIGHEST, preferred_element_type=F32)
    sep_rows = lax.dynamic_slice_in_dim(delta, first_row, owned, 0)
    mixed, contrib = call(
        middle_kernel,
        [jax.ShapeDtypeStruct(leaf_load.shape, F32), jax.ShapeDtypeStruct(contrib.shape, F32)],
        delta,
        columns,
        leaf_matrix,
        leaf_inverse,
        leaf_load,
        cubic_coeff[:, None],
        solved,
    )
    delta = correction(contrib, local, inverse_rows, place)
    leaf_state = call(
        end_kernel, jax.ShapeDtypeStruct(leaf_load.shape, F32), delta, columns, leaf_inverse, mixed
    )
    sep_rows = sep_rows + lax.dynamic_slice_in_dim(delta, first_row, owned, 0)
    return leaf_state, sep_rows


def solution(mesh):
    grid = Mesh(mesh.devices.reshape(NX, NY, NZ, NC), ("x", "y", "z", "c"))
    leaf = ("x", "y", "z")
    in_specs = (
        P(leaf, None),
        P(leaf, None),
        P(leaf, None),
        P(leaf),
        P(leaf, "c"),
        P(leaf, "c"),
        P(leaf + ("c",), None),
        P(leaf + ("c",), None),
        P(),
        P(leaf, None),
    )
    out_specs = (P(leaf, "c"), P(leaf, "c"))
    return jax.shard_map(on_device, mesh=grid, in_specs=in_specs, out_specs=out_specs, check_vma=False)
```

```python
import jax
import jax.numpy as jnp
from jax import lax
from jax.experimental import pallas as pl
from jax.experimental.pallas import tpu as pltpu
from jax.sharding import Mesh, PartitionSpec as P

BLOCK = 128
NX, NY, NZ, NC = 4, 4, 16, 2
NXY = NX * NY
OWN = 4
TILE = 512
START_MIB = 24
MIDDLE_MIB = 14
F32 = jnp.float32
BF16 = jnp.bfloat16
HIGHEST = lax.Precision.HIGHEST
MIB = 1024 * 1024
HBM = pl.BlockSpec(memory_space=pltpu.HBM)
SMEM = pl.BlockSpec(memory_space=pltpu.SMEM)
VMEM = pl.BlockSpec(memory_space=pltpu.VMEM)
DMA = pltpu.SemaphoreType.DMA


def dot(left, right):
    return jnp.dot(left, right, preferred_element_type=F32)


def f32(*shape):
    return jax.ShapeDtypeStruct(shape, F32)


def far(shape, dtype=F32):
    return pltpu.HBM(shape, dtype)


def call(kernel, out_shape, out_specs, in_specs, scratch, limit, *args):
    args = [pltpu.with_memory_space_constraint(x, pltpu.HBM) if spec is HBM else x for spec, x in zip(in_specs, args)]
    return pl.pallas_call(
        kernel,
        out_shape=out_shape,
        out_specs=out_specs,
        in_specs=in_specs,
        scratch_shapes=scratch,
        compiler_params=pltpu.CompilerParams(vmem_limit_bytes=limit * MIB),
    )(*args)


def fetch(sources, targets, sems):
    copies = [pltpu.make_async_copy(s, t, sems.at[i]) for i, (s, t) in enumerate(zip(sources, targets))]
    for copy in copies:
        copy.start()
    return copies


def send_tile(part, tile, scratch, contrib, sems):
    count = part.shape[1] // BLOCK
    first = tile * count
    for i in range(count):
        scratch[first + i] = part[:, i * BLOCK : (i + 1) * BLOCK]
    rows = pl.ds(first, count)
    copy = pltpu.make_async_copy(scratch.at[rows], contrib.at[rows], sems.at[tile])
    copy.start()
    return copy


def start_kernel(
    mask_in, inverse_in, load_in, owner_in, coupling_in, columns_out, solved_out, contrib,
    mask, inverse, load, owner, coupling, columns, solved, part_buf, in_sems, out_sems, part_sems,
):
    waits = fetch(
        (mask_in, inverse_in, load_in, owner_in, coupling_in), (mask, inverse, load, owner, coupling), in_sems
    )
    for wait in waits[:3]:
        wait.wait()
    solved[...] = dot(inverse[...], load[...].astype(BF16))
    copies = [pltpu.make_async_copy(solved, solved_out, out_sems.at[0])]
    copies[0].start()
    mixed_t = solved[...].T.astype(BF16)
    for wait in waits[3:]:
        wait.wait()
    for i in range(coupling.shape[1] // BLOCK):
        cols = slice(i * BLOCK, (i + 1) * BLOCK)
        coupling[:, cols] = jnp.where(mask[0, i] != 0, coupling[:, cols], jnp.zeros((), BF16))
    for tile in range(coupling.shape[1] // TILE):
        cols = pl.ds(tile * TILE, TILE)
        rows = lax.broadcasted_iota(jnp.int32, (coupling.shape[1], TILE), 0)
        pick = (rows == owner[:, cols]).astype(BF16)
        picked = dot(coupling[...], pick).astype(BF16)
        columns[:, cols] = picked
        copy = pltpu.make_async_copy(columns.at[:, cols], columns_out.at[:, cols], out_sems.at[1 + tile])
        copy.start()
        copies.append(copy)
        copies.append(send_tile(dot(mixed_t, picked), tile, part_buf, contrib, part_sems))
    for copy in copies:
        copy.wait()


def start(mask, inverse, coupling, load, owner):
    width, sep_width = coupling.shape
    cases = load.shape[1]
    tiles = sep_width // TILE
    return call(
        start_kernel,
        [far((width, sep_width), BF16), far((width, cases)), far((NXY, cases, BLOCK))],
        [HBM, HBM, HBM],
        [HBM] * 5,
        [
            pltpu.SMEM(mask.shape, jnp.int32),
            pltpu.VMEM(inverse.shape, BF16),
            pltpu.VMEM(load.shape, F32),
            pltpu.VMEM(owner.shape, jnp.int32),
            pltpu.VMEM(coupling.shape, BF16),
            pltpu.VMEM(coupling.shape, BF16),
            pltpu.VMEM(load.shape, F32),
            pltpu.VMEM((NXY, cases, BLOCK), F32),
            DMA((5,)),
            DMA((1 + tiles,)),
            DMA((tiles,)),
        ],
        START_MIB,
        mask, inverse, load, owner, coupling,
    )


def pack_sum_kernel(parts, local_t, packed, out, buf, sem):
    group = parts.shape[1] // NZ
    total = local_t[...] - jnp.sum(parts[...], axis=0)
    for z in range(NZ):
        buf[z, :group] = total[z * group : (z + 1) * group]
        buf[z, group:] = packed[...]
    copy = pltpu.make_async_copy(buf, out, sem)
    copy.start()
    copy.wait()


def sum_rows_kernel(parts, local_t, out):
    total = local_t[...] - jnp.sum(parts[...], axis=0)
    out[...] = total.reshape(out.shape)


def sum_cases_kernel(parts, out):
    total = jnp.sum(parts[:, : out.shape[1]], axis=0)
    out[...] = jnp.broadcast_to(total[None], out.shape)


def delta_kernel(core, rhs, mine, other, out):
    group, sub = rhs.shape[1], OWN
    acc_mine = jnp.zeros((2 * group, BLOCK), F32)
    acc_other = jnp.zeros((2 * group, BLOCK), F32)
    for i in range(NXY // 2):
        left = rhs[2 * i : 2 * i + 2].reshape(2 * group, BLOCK)
        rows = slice(group + 2 * sub * i, group + 2 * sub * (i + 1))
        acc_mine = acc_mine + rows_dot(left, mine[:, rows].reshape(BLOCK, BLOCK))
        acc_other = acc_other + rows_dot(left, other[:, rows].reshape(BLOCK, BLOCK))
    low = lax.broadcasted_iota(jnp.int32, (group, BLOCK), 1) % (2 * sub) < sub

    def pair(acc):
        return jnp.where(low, acc[:group] + pltpu.roll(acc[group:], BLOCK - sub, 1), 0.0)

    own, far = pair(acc_mine), pair(acc_other)
    first = core[0] == 0
    total = jnp.where(first, own, far) + pltpu.roll(jnp.where(first, far, own), sub, 1)
    out[...] = jnp.broadcast_to(total[None], out.shape)


def rows_dot(left, rows):
    return lax.dot_general(
        left, rows, (((1,), (1,)), ((), ())), precision=HIGHEST, preferred_element_type=F32
    )


def spread_kernel(parts, out, buf, sems):
    buf[...] = parts[...].reshape(buf.shape[1], BLOCK).T
    copies = [pltpu.make_async_copy(buf, out.at[i], sems.at[i]) for i in range(NXY)]
    for copy in copies:
        copy.start()
    for copy in copies:
        copy.wait()


def coupled_product(columns_in, columns, delta, sems):
    width, sep_width = columns.shape
    total = jnp.zeros((width, delta.shape[1]), F32)
    for tile in range(sep_width // TILE):
        cols = pl.ds(tile * TILE, TILE)
        pltpu.make_async_copy(columns_in.at[:, cols], columns.at[:, cols], sems.at[tile]).wait()
        total = total + dot(columns[:, cols], delta[cols, :].astype(BF16))
    return total


def fetch_columns(columns_in, columns, sems):
    for tile in range(columns.shape[1] // TILE):
        cols = pl.ds(tile * TILE, TILE)
        pltpu.make_async_copy(columns_in.at[:, cols], columns.at[:, cols], sems.at[tile]).start()


def middle_kernel(
    delta, cubic, columns_in, inverse_in, solved_in, matrix_in, load_in, state_out, contrib,
    columns, inverse, solved, matrix, load, mixed, part_buf, col_sems, in_sems, out_sem, part_sems,
):
    fetch_columns(columns_in, columns, col_sems)
    waits = fetch((inverse_in, solved_in, matrix_in, load_in), (inverse, solved, matrix, load), in_sems)
    coupled = coupled_product(columns_in, columns, delta, col_sems)
    waits[0].wait()
    waits[1].wait()
    state = solved[...] - dot(inverse[...], coupled.astype(BF16))
    waits[2].wait()
    waits[3].wait()
    resid = load[...] - dot(matrix[...], state.astype(BF16)) - coupled
    resid = resid - cubic[...] * state * state * state
    mixed[...] = state + dot(inverse[...], resid.astype(BF16))
    copies = [pltpu.make_async_copy(mixed, state_out, out_sem)]
    copies[0].start()
    mixed_t = mixed[...].T.astype(BF16)
    for tile in range(columns.shape[1] // TILE):
        part = dot(mixed_t, columns[:, tile * TILE : (tile + 1) * TILE])
        copies.append(send_tile(part, tile, part_buf, contrib, part_sems))
    for copy in copies:
        copy.wait()


def end_kernel(delta, columns_in, inverse_in, mixed_in, out, columns, inverse, mixed, state, col_sems, in_sems, out_sems):
    fetch_columns(columns_in, columns, col_sems)
    waits = fetch((inverse_in, mixed_in), (inverse, mixed), in_sems)
    back = coupled_product(columns_in, columns, delta, col_sems).astype(BF16)
    for wait in waits:
        wait.wait()
    count = out_sems.shape[0]
    rows = state.shape[0] // count
    copies = []
    for i in range(count):
        part = pl.ds(i * rows, rows)
        state[part, :] = mixed[part, :] - dot(inverse[part, :], back)
        copy = pltpu.make_async_copy(state.at[part], out.at[part], out_sems.at[i])
        copy.start()
        copies.append(copy)
    for copy in copies:
        copy.wait()


def exchange(parts, axes):
    return lax.all_to_all(parts, axes, 0, 0, tiled=True)


def correction(contrib, local, place, core, packed, rows):
    cases = contrib.shape[1]
    group = cases // NZ
    local_t = lax.dynamic_update_slice_in_dim(jnp.zeros((BLOCK, cases), F32), local, place, 0).T
    parts = exchange(contrib, ("x", "y"))
    if rows is None:
        sent = (NZ, group + packed.shape[0], BLOCK)
        parts = call(
            pack_sum_kernel, far(sent), HBM, [VMEM] * 3, [pltpu.VMEM(sent, F32), DMA], 8, parts, local_t, packed
        )
        parts = exchange(parts, "z")
        rows = (parts, lax.ppermute(parts, "c", [(0, 1), (1, 0)]))
    else:
        parts = call(sum_rows_kernel, f32(NZ, group, BLOCK), VMEM, [VMEM] * 2, [], 8, parts, local_t)
        parts = exchange(parts, "z")
    rhs = call(sum_cases_kernel, f32(NXY, group, BLOCK), VMEM, [VMEM], [], 4, parts)
    rhs = exchange(rhs, ("x", "y"))
    delta = call(delta_kernel, f32(NZ, group, BLOCK), VMEM, [SMEM] + [VMEM] * 3, [], 8, core, rhs, *rows)
    delta = exchange(delta, "z")
    delta = call(
        spread_kernel,
        far((NXY, BLOCK, cases)),
        HBM,
        [VMEM],
        [pltpu.VMEM((BLOCK, cases), F32), DMA((NXY,))],
        4,
        delta,
    )
    return exchange(delta, ("x", "y")).reshape(NXY * BLOCK, cases), rows


def on_device(
    leaf_matrix,
    leaf_inverse,
    coupling,
    cubic_coeff,
    leaf_load,
    sep_load,
    sep_matrix,
    sep_inverse,
    owner_map,
    block_mask,
):
    owned, cases = sep_load.shape
    width, sep_width = coupling.shape
    matrix_rows = lax.all_gather(sep_matrix, "c", axis=0, tiled=True)
    packed = sep_inverse.reshape(OWN, NXY, BLOCK).transpose(1, 0, 2).reshape(OWN * NXY, BLOCK)
    core = lax.axis_index("c").astype(jnp.int32)[None]
    place = lax.axis_index("z") * owned
    first_row = lax.axis_index(("x", "y", "z")) * owned
    columns, solved, contrib = start(block_mask, leaf_inverse, coupling, leaf_load, owner_map[None, :])

    delta, rows = correction(contrib, sep_load, place, core, packed, None)
    local = sep_load - jnp.dot(matrix_rows, delta, precision=HIGHEST, preferred_element_type=F32)
    sep_rows = lax.dynamic_slice_in_dim(delta, first_row, owned, 0)
    tiles = sep_width // TILE
    mixed, contrib = call(
        middle_kernel,
        [far((width, cases)), far((NXY, cases, BLOCK))],
        [HBM, HBM],
        [VMEM, VMEM] + [HBM] * 5,
        [
            pltpu.VMEM(columns.shape, BF16),
            pltpu.VMEM(leaf_inverse.shape, BF16),
            pltpu.VMEM(solved.shape, F32),
            pltpu.VMEM(leaf_matrix.shape, BF16),
            pltpu.VMEM(leaf_load.shape, F32),
            pltpu.VMEM(solved.shape, F32),
            pltpu.VMEM((NXY, cases, BLOCK), F32),
            DMA((tiles,)),
            DMA((4,)),
            DMA,
            DMA((tiles,)),
        ],
        MIDDLE_MIB,
        delta, cubic_coeff[:, None], columns, leaf_inverse, solved, leaf_matrix, leaf_load,
    )
    delta, rows = correction(contrib, local, place, core, packed, rows)
    leaf_state = call(
        end_kernel,
        far((width, cases)),
        HBM,
        [VMEM] + [HBM] * 3,
        [
            pltpu.VMEM(columns.shape, BF16),
            pltpu.VMEM(leaf_inverse.shape, BF16),
            pltpu.VMEM(mixed.shape, F32),
            pltpu.VMEM(mixed.shape, F32),
            DMA((tiles,)),
            DMA((2,)),
            DMA((2,)),
        ],
        MIDDLE_MIB,
        delta, columns, leaf_inverse, mixed,
    )
    sep_rows = sep_rows + lax.dynamic_slice_in_dim(delta, first_row, owned, 0)
    return leaf_state, sep_rows


def solution(mesh):
    grid = Mesh(mesh.devices.reshape(NX, NY, NZ, NC), ("x", "y", "z", "c"))
    leaf = ("x", "y", "z")
    in_specs = (
        P(leaf, None),
        P(leaf, None),
        P(leaf, None),
        P(leaf),
        P(leaf, "c"),
        P(leaf, "c"),
        P(leaf + ("c",), None),
        P(leaf + ("c",), None),
        P(),
        P(leaf, None),
    )
    out_specs = (P(leaf, "c"), P(leaf, "c"))
    return jax.shard_map(on_device, mesh=grid, in_specs=in_specs, out_specs=out_specs, check_vma=False)
```

```python
import jax
import jax.numpy as jnp
from jax import lax
from jax.experimental import pallas as pl
from jax.experimental.pallas import tpu as pltpu
from jax.sharding import Mesh, PartitionSpec as P

BLOCK = 128
NX, NY, NZ, NC = 4, 4, 16, 2
NXY = NX * NY
OWN = 4
SPLIT = 2
PART = OWN // SPLIT
TILE = 512
START_MIB = 24
MIDDLE_MIB = 14
F32 = jnp.float32
BF16 = jnp.bfloat16
HIGHEST = lax.Precision.HIGHEST
MIB = 1024 * 1024
HBM = pl.BlockSpec(memory_space=pltpu.HBM)
SMEM = pl.BlockSpec(memory_space=pltpu.SMEM)
VMEM = pl.BlockSpec(memory_space=pltpu.VMEM)
DMA = pltpu.SemaphoreType.DMA


def dot(left, right):
    return jnp.dot(left, right, preferred_element_type=F32)


def f32(*shape):
    return jax.ShapeDtypeStruct(shape, F32)


def far(shape, dtype=F32):
    return pltpu.HBM(shape, dtype)


def call(kernel, out_shape, out_specs, in_specs, scratch, limit, *args):
    args = [pltpu.with_memory_space_constraint(x, pltpu.HBM) if spec is HBM else x for spec, x in zip(in_specs, args)]
    return pl.pallas_call(
        kernel,
        out_shape=out_shape,
        out_specs=out_specs,
        in_specs=in_specs,
        scratch_shapes=scratch,
        compiler_params=pltpu.CompilerParams(vmem_limit_bytes=limit * MIB),
    )(*args)


def fetch(sources, targets, sems):
    copies = [pltpu.make_async_copy(s, t, sems.at[i]) for i, (s, t) in enumerate(zip(sources, targets))]
    for copy in copies:
        copy.start()
    return copies


def send_tile(part, tile, scratch, contrib, sems):
    count = part.shape[1] // BLOCK
    first = tile * count
    for i in range(count):
        scratch[first + i] = part[:, i * BLOCK : (i + 1) * BLOCK]
    rows = pl.ds(first, count)
    copy = pltpu.make_async_copy(scratch.at[rows], contrib.at[rows], sems.at[tile])
    copy.start()
    return copy


def start_kernel(
    mask_in, inverse_in, load_in, owner_in, coupling_in, columns_out, solved_out, contrib,
    mask, inverse, load, owner, coupling, columns, solved, part_buf, in_sems, out_sems, part_sems,
):
    waits = fetch(
        (mask_in, inverse_in, load_in, owner_in, coupling_in), (mask, inverse, load, owner, coupling), in_sems
    )
    for wait in waits[:3]:
        wait.wait()
    solved[...] = dot(inverse[...], load[...].astype(BF16))
    copies = [pltpu.make_async_copy(solved, solved_out, out_sems.at[0])]
    copies[0].start()
    mixed_t = solved[...].T.astype(BF16)
    for wait in waits[3:]:
        wait.wait()
    for i in range(coupling.shape[1] // BLOCK):
        cols = slice(i * BLOCK, (i + 1) * BLOCK)
        coupling[:, cols] = jnp.where(mask[0, i] != 0, coupling[:, cols], jnp.zeros((), BF16))
    for tile in range(coupling.shape[1] // TILE):
        cols = pl.ds(tile * TILE, TILE)
        rows = lax.broadcasted_iota(jnp.int32, (coupling.shape[1], TILE), 0)
        pick = (rows == owner[:, cols]).astype(BF16)
        picked = dot(coupling[...], pick).astype(BF16)
        columns[:, cols] = picked
        copy = pltpu.make_async_copy(columns.at[:, cols], columns_out.at[:, cols], out_sems.at[1 + tile])
        copy.start()
        copies.append(copy)
        copies.append(send_tile(dot(mixed_t, picked), tile, part_buf, contrib, part_sems))
    for copy in copies:
        copy.wait()


def start(mask, inverse, coupling, load, owner):
    width, sep_width = coupling.shape
    cases = load.shape[1]
    tiles = sep_width // TILE
    return call(
        start_kernel,
        [far((width, sep_width), BF16), far((width, cases)), far((NXY, cases, BLOCK))],
        [HBM, HBM, HBM],
        [HBM] * 5,
        [
            pltpu.SMEM(mask.shape, jnp.int32),
            pltpu.VMEM(inverse.shape, BF16),
            pltpu.VMEM(load.shape, F32),
            pltpu.VMEM(owner.shape, jnp.int32),
            pltpu.VMEM(coupling.shape, BF16),
            pltpu.VMEM(coupling.shape, BF16),
            pltpu.VMEM(load.shape, F32),
            pltpu.VMEM((NXY, cases, BLOCK), F32),
            DMA((5,)),
            DMA((1 + tiles,)),
            DMA((tiles,)),
        ],
        START_MIB,
        mask, inverse, load, owner, coupling,
    )


def case_group(total, z):
    group = total.shape[0] * SPLIT // NZ
    first = z // SPLIT * group
    return total[first : first + group]


def pack_sum_kernel(parts, local_t, packed, out, buf, sem):
    group = parts.shape[1] * SPLIT // NZ
    total = local_t[...] - jnp.sum(parts[...], axis=0)
    for z in range(NZ):
        buf[z, :group] = case_group(total, z)
        buf[z, group:] = packed[z % SPLIT]
    copy = pltpu.make_async_copy(buf, out, sem)
    copy.start()
    copy.wait()


def sum_rows_kernel(parts, local_t, out):
    total = local_t[...] - jnp.sum(parts[...], axis=0)
    for z in range(NZ):
        out[z] = case_group(total, z)


def sum_cases_kernel(parts, out):
    total = jnp.sum(parts[:, : out.shape[1]], axis=0)
    out[...] = jnp.broadcast_to(total[None], out.shape)


def delta_kernel(core, rhs, mine, other, out):
    cases = rhs.shape[1]
    span = BLOCK // (NZ * PART)
    base = mine.shape[1] - NXY * PART
    acc_mine = jnp.zeros((span * cases, BLOCK), F32)
    acc_other = jnp.zeros((span * cases, BLOCK), F32)
    for i in range(NXY // span):
        left = rhs[span * i : span * (i + 1)].reshape(span * cases, BLOCK)
        rows = slice(base + 8 * i, base + 8 * (i + 1))
        acc_mine = acc_mine + rows_dot(left, mine[:, rows].reshape(BLOCK, BLOCK))
        acc_other = acc_other + rows_dot(left, other[:, rows].reshape(BLOCK, BLOCK))
    low = lax.broadcasted_iota(jnp.int32, (cases, BLOCK), 1) % 8 < PART

    def fold(acc):
        total = acc[:cases]
        for j in range(1, span):
            total = total + pltpu.roll(acc[j * cases : (j + 1) * cases], BLOCK - PART * j, 1)
        return jnp.where(low, total, 0.0)

    own, far_rows = fold(acc_mine), fold(acc_other)
    first = core[0] == 0
    total = jnp.where(first, own, far_rows) + pltpu.roll(jnp.where(first, far_rows, own), OWN, 1)
    half = cases // SPLIT
    tile = total[:half] + pltpu.roll(total[half:], PART, 1)
    out[...] = jnp.broadcast_to(tile[None], out.shape)


def rows_dot(left, rows):
    return lax.dot_general(
        left, rows, (((1,), (1,)), ((), ())), precision=HIGHEST, preferred_element_type=F32
    )


def spread_kernel(parts, out, cases_buf, buf, sems):
    half = parts.shape[1]
    low = lax.broadcasted_iota(jnp.int32, (half, BLOCK), 1) % (2 * PART) < PART
    for i in range(NZ // SPLIT):
        even, odd = parts[SPLIT * i], parts[SPLIT * i + 1]
        cases_buf[2 * half * i : 2 * half * i + half] = jnp.where(low, even, pltpu.roll(odd, PART, 1))
        cases_buf[2 * half * i + half : 2 * half * (i + 1)] = jnp.where(low, pltpu.roll(even, BLOCK - PART, 1), odd)
    buf[...] = cases_buf[...].T
    copies = [pltpu.make_async_copy(buf, out.at[i], sems.at[i]) for i in range(NXY)]
    for copy in copies:
        copy.start()
    for copy in copies:
        copy.wait()


def coupled_product(columns_in, columns, delta, sems):
    width, sep_width = columns.shape
    total = jnp.zeros((width, delta.shape[1]), F32)
    for tile in range(sep_width // TILE):
        cols = pl.ds(tile * TILE, TILE)
        pltpu.make_async_copy(columns_in.at[:, cols], columns.at[:, cols], sems.at[tile]).wait()
        total = total + dot(columns[:, cols], delta[cols, :].astype(BF16))
    return total


def fetch_columns(columns_in, columns, sems):
    for tile in range(columns.shape[1] // TILE):
        cols = pl.ds(tile * TILE, TILE)
        pltpu.make_async_copy(columns_in.at[:, cols], columns.at[:, cols], sems.at[tile]).start()


def middle_kernel(
    delta, cubic, columns_in, inverse_in, solved_in, matrix_in, load_in, state_out, contrib,
    columns, inverse, solved, matrix, load, mixed, part_buf, col_sems, in_sems, out_sem, part_sems,
):
    fetch_columns(columns_in, columns, col_sems)
    waits = fetch((inverse_in, solved_in, matrix_in, load_in), (inverse, solved, matrix, load), in_sems)
    coupled = coupled_product(columns_in, columns, delta, col_sems)
    waits[0].wait()
    waits[1].wait()
    state = solved[...] - dot(inverse[...], coupled.astype(BF16))
    waits[2].wait()
    waits[3].wait()
    resid = load[...] - dot(matrix[...], state.astype(BF16)) - coupled
    resid = resid - cubic[...] * state * state * state
    mixed[...] = state + dot(inverse[...], resid.astype(BF16))
    copies = [pltpu.make_async_copy(mixed, state_out, out_sem)]
    copies[0].start()
    mixed_t = mixed[...].T.astype(BF16)
    for tile in range(columns.shape[1] // TILE):
        part = dot(mixed_t, columns[:, tile * TILE : (tile + 1) * TILE])
        copies.append(send_tile(part, tile, part_buf, contrib, part_sems))
    for copy in copies:
        copy.wait()


def end_kernel(delta, columns_in, inverse_in, mixed_in, out, columns, inverse, mixed, state, col_sems, in_sems, out_sems):
    fetch_columns(columns_in, columns, col_sems)
    waits = fetch((inverse_in, mixed_in), (inverse, mixed), in_sems)
    back = coupled_product(columns_in, columns, delta, col_sems).astype(BF16)
    for wait in waits:
        wait.wait()
    count = out_sems.shape[0]
    rows = state.shape[0] // count
    copies = []
    for i in range(count):
        part = pl.ds(i * rows, rows)
        state[part, :] = mixed[part, :] - dot(inverse[part, :], back)
        copy = pltpu.make_async_copy(state.at[part], out.at[part], out_sems.at[i])
        copy.start()
        copies.append(copy)
    for copy in copies:
        copy.wait()


def exchange(parts, axes):
    return lax.all_to_all(parts, axes, 0, 0, tiled=True)


def correction(contrib, local, place, core, packed, rows):
    cases = contrib.shape[1]
    group = cases * SPLIT // NZ
    local_t = lax.dynamic_update_slice_in_dim(jnp.zeros((BLOCK, cases), F32), local, place, 0).T
    parts = exchange(contrib, ("x", "y"))
    first = rows is None
    if first:
        sent = (NZ, group + packed.shape[1], BLOCK)
        parts = call(
            pack_sum_kernel, far(sent), HBM, [VMEM] * 3, [pltpu.VMEM(sent, F32), DMA], 8, parts, local_t, packed
        )
    else:
        parts = call(sum_rows_kernel, f32(NZ, group, BLOCK), VMEM, [VMEM] * 2, [], 8, parts, local_t)
    parts = exchange(parts, "z")
    rhs = call(sum_cases_kernel, f32(NXY, group, BLOCK), VMEM, [VMEM], [], 4, parts)
    if first:
        parts, rhs = lax.optimization_barrier((parts, rhs))
        rows = (parts, lax.ppermute(parts, "c", [(0, 1), (1, 0)]))
    rhs = exchange(rhs, ("x", "y"))
    delta = call(
        delta_kernel, f32(NZ, group // SPLIT, BLOCK), VMEM, [SMEM] + [VMEM] * 3, [], 8, core, rhs, *rows
    )
    delta = exchange(delta, "z")
    delta = call(
        spread_kernel,
        far((NXY, BLOCK, cases)),
        HBM,
        [VMEM],
        [pltpu.VMEM((cases, BLOCK), F32), pltpu.VMEM((BLOCK, cases), F32), DMA((NXY,))],
        4,
        delta,
    )
    return exchange(delta, ("x", "y")).reshape(NXY * BLOCK, cases), rows


def on_device(
    leaf_matrix,
    leaf_inverse,
    coupling,
    cubic_coeff,
    leaf_load,
    sep_load,
    sep_matrix,
    sep_inverse,
    owner_map,
    block_mask,
):
    owned, cases = sep_load.shape
    width, sep_width = coupling.shape
    matrix_rows = lax.all_gather(sep_matrix, "c", axis=0, tiled=True)
    packed = sep_inverse.reshape(SPLIT, PART, NXY, BLOCK).transpose(0, 2, 1, 3).reshape(SPLIT, NXY * PART, BLOCK)
    core = lax.axis_index("c").astype(jnp.int32)[None]
    place = lax.axis_index("z") * owned
    first_row = lax.axis_index(("x", "y", "z")) * owned
    columns, solved, contrib = start(block_mask, leaf_inverse, coupling, leaf_load, owner_map[None, :])

    delta, rows = correction(contrib, sep_load, place, core, packed, None)
    local = sep_load - jnp.dot(matrix_rows, delta, precision=HIGHEST, preferred_element_type=F32)
    sep_rows = lax.dynamic_slice_in_dim(delta, first_row, owned, 0)
    tiles = sep_width // TILE
    mixed, contrib = call(
        middle_kernel,
        [far((width, cases)), far((NXY, cases, BLOCK))],
        [HBM, HBM],
        [VMEM, VMEM] + [HBM] * 5,
        [
            pltpu.VMEM(columns.shape, BF16),
            pltpu.VMEM(leaf_inverse.shape, BF16),
            pltpu.VMEM(solved.shape, F32),
            pltpu.VMEM(leaf_matrix.shape, BF16),
            pltpu.VMEM(leaf_load.shape, F32),
            pltpu.VMEM(solved.shape, F32),
            pltpu.VMEM((NXY, cases, BLOCK), F32),
            DMA((tiles,)),
            DMA((4,)),
            DMA,
            DMA((tiles,)),
        ],
        MIDDLE_MIB,
        delta, cubic_coeff[:, None], columns, leaf_inverse, solved, leaf_matrix, leaf_load,
    )
    delta, rows = correction(contrib, local, place, core, packed, rows)
    leaf_state = call(
        end_kernel,
        far((width, cases)),
        HBM,
        [VMEM] + [HBM] * 3,
        [
            pltpu.VMEM(columns.shape, BF16),
            pltpu.VMEM(leaf_inverse.shape, BF16),
            pltpu.VMEM(mixed.shape, F32),
            pltpu.VMEM(mixed.shape, F32),
            DMA((tiles,)),
            DMA((2,)),
            DMA((2,)),
        ],
        MIDDLE_MIB,
        delta, columns, leaf_inverse, mixed,
    )
    sep_rows = sep_rows + lax.dynamic_slice_in_dim(delta, first_row, owned, 0)
    return leaf_state, sep_rows


def solution(mesh):
    grid = Mesh(mesh.devices.reshape(NX, NY, NZ, NC), ("x", "y", "z", "c"))
    leaf = ("x", "y", "z")
    in_specs = (
        P(leaf, None),
        P(leaf, None),
        P(leaf, None),
        P(leaf),
        P(leaf, "c"),
        P(leaf, "c"),
        P(leaf + ("c",), None),
        P(leaf + ("c",), None),
        P(),
        P(leaf, None),
    )
    out_specs = (P(leaf, "c"), P(leaf, "c"))
    return jax.shard_map(on_device, mesh=grid, in_specs=in_specs, out_specs=out_specs, check_vma=False)
```

```python
import jax
import jax.numpy as jnp
from jax import lax
from jax.experimental import pallas as pl
from jax.experimental.pallas import tpu as pltpu
from jax.sharding import Mesh, PartitionSpec as P

BLOCK = 128
NX, NY, NZ, NC = 4, 4, 16, 2
NXY = NX * NY
OWN = 4
SPLIT = 2
PART = OWN // SPLIT
TILE = 512
OUT_TILES = 4
START_MIB = 16
PERMUTE_MIB = 32
MIDDLE_MIB = 14
F32 = jnp.float32
BF16 = jnp.bfloat16
HIGHEST = lax.Precision.HIGHEST
MIB = 1024 * 1024
HBM = pl.BlockSpec(memory_space=pltpu.HBM)
SMEM = pl.BlockSpec(memory_space=pltpu.SMEM)
VMEM = pl.BlockSpec(memory_space=pltpu.VMEM)
DMA = pltpu.SemaphoreType.DMA


def dot(left, right):
    return jnp.dot(left, right, preferred_element_type=F32)


def f32(*shape):
    return jax.ShapeDtypeStruct(shape, F32)


def far(shape, dtype=F32):
    return pltpu.HBM(shape, dtype)


def call(kernel, out_shape, out_specs, in_specs, scratch, limit, *args):
    args = [pltpu.with_memory_space_constraint(x, pltpu.HBM) if spec is HBM else x for spec, x in zip(in_specs, args)]
    return pl.pallas_call(
        kernel,
        out_shape=out_shape,
        out_specs=out_specs,
        in_specs=in_specs,
        scratch_shapes=scratch,
        compiler_params=pltpu.CompilerParams(vmem_limit_bytes=limit * MIB),
    )(*args)


def fetch(sources, targets, sems):
    copies = [pltpu.make_async_copy(s, t, sems.at[i]) for i, (s, t) in enumerate(zip(sources, targets))]
    for copy in copies:
        copy.start()
    return copies


def send_tile(part, tile, scratch, contrib, sems):
    count = part.shape[1] // BLOCK
    first = tile * count
    for i in range(count):
        scratch[first + i] = part[:, i * BLOCK : (i + 1) * BLOCK]
    rows = pl.ds(first, count)
    copy = pltpu.make_async_copy(scratch.at[rows], contrib.at[rows], sems.at[tile])
    copy.start()
    return copy


def masked(mask, coupling):
    for i in range(coupling.shape[1] // BLOCK):
        cols = slice(i * BLOCK, (i + 1) * BLOCK)
        coupling[:, cols] = jnp.where(mask[0, i] != 0, coupling[:, cols], jnp.zeros((), BF16))


def picks(owner, tile, size):
    rows = lax.broadcasted_iota(jnp.int32, (owner.shape[1], size), 0)
    return (rows == owner[:, tile * size : (tile + 1) * size]).astype(BF16)


def split3(x):
    high = x.astype(BF16)
    rest = x - high.astype(F32)
    mid = rest.astype(BF16)
    return [high, mid, (rest - mid.astype(F32)).astype(BF16)]


def start_kernel(
    first, mask_in, inverse_in, load_in, owner_in, sep_in, coupling_in, solved_out, contrib,
    mask, inverse, load, owner, sep, coupling, solved, part_buf, in_sems, out_sem, part_sems,
):
    waits = fetch(
        (mask_in, inverse_in, load_in, owner_in, sep_in, coupling_in),
        (mask, inverse, load, owner, sep, coupling),
        in_sems,
    )
    for wait in waits[1:3]:
        wait.wait()
    solved[...] = dot(inverse[...], load[...].astype(BF16))
    copies = [pltpu.make_async_copy(solved, solved_out, out_sem)]
    copies[0].start()
    mixed_t = solved[...].T.astype(BF16)
    for wait in waits[:1] + waits[3:]:
        wait.wait()
    masked(mask, coupling)
    own, sep_width = sep.shape[0], coupling.shape[1]
    size = sep_width // part_sems.shape[0]
    index = lax.broadcasted_iota(jnp.int32, (own, size), 0)
    target = jnp.zeros((own, size), jnp.int32)
    for j in range(own):
        target = jnp.where(index == j, owner[0, first[0] + j], target)
    for tile in range(part_sems.shape[0]):
        lanes = lax.broadcasted_iota(jnp.int32, (own, size), 1) + tile * size
        place = (lanes == target).astype(F32)
        loads = lax.dot_general(
            sep[...], place, (((0,), (0,)), ((), ())), precision=HIGHEST, preferred_element_type=F32
        )
        part = dot(mixed_t, coupling[:, tile * size : (tile + 1) * size]) - loads
        copies.append(send_tile(part, tile, part_buf, contrib, part_sems))
    for copy in copies:
        copy.wait()


def start(first, mask, inverse, coupling, load, owner, sep):
    cases = load.shape[1]
    return call(
        start_kernel,
        [far(load.shape), far((NXY, cases, BLOCK))],
        [HBM] * 2,
        [SMEM] + [HBM] * 6,
        [
            pltpu.SMEM(mask.shape, jnp.int32),
            pltpu.VMEM(inverse.shape, BF16),
            pltpu.VMEM(load.shape, F32),
            pltpu.SMEM(owner.shape, jnp.int32),
            pltpu.VMEM(sep.shape, F32),
            pltpu.VMEM(coupling.shape, BF16),
            pltpu.VMEM(load.shape, F32),
            pltpu.VMEM((NXY, cases, BLOCK), F32),
            DMA((6,)),
            DMA,
            DMA((OUT_TILES,)),
        ],
        START_MIB,
        first, mask, inverse, load, owner, sep, coupling,
    )


def permute_kernel(
    mask_in, owner_in, own_in, coupling_in, after, columns_out, packed,
    mask, owner, own, coupling, columns, in_sems, out_sems,
):
    waits = fetch((mask_in, owner_in, own_in, coupling_in), (mask, owner, own, coupling), in_sems)
    for wait in waits:
        wait.wait()
    masked(mask, coupling)
    terms = jnp.concatenate([x.astype(F32) for x in split3(own[...])], axis=0).astype(BF16)
    rows = jnp.zeros((3 * OWN, owner.shape[1]), F32)
    copies = []
    for tile in range(coupling.shape[1] // TILE):
        cols = pl.ds(tile * TILE, TILE)
        pick = picks(owner, tile, TILE)
        columns[:, cols] = dot(coupling[...], pick).astype(BF16)
        copy = pltpu.make_async_copy(columns.at[:, cols], columns_out.at[:, cols], out_sems.at[tile])
        copy.start()
        copies.append(copy)
        rows = rows + lax.dot_general(
            terms[:, tile * TILE : (tile + 1) * TILE], pick, (((1,), (1,)), ((), ())), preferred_element_type=F32
        )
    rows = rows[:OWN] + rows[OWN : 2 * OWN] + rows[2 * OWN :]
    for k in range(SPLIT):
        for t in range(NXY):
            packed[k, t * PART : (t + 1) * PART] = rows[k * PART : (k + 1) * PART, t * BLOCK : (t + 1) * BLOCK]
    for copy in copies:
        copy.wait()


def permute(mask, owner, own, coupling, after):
    return call(
        permute_kernel,
        [far(coupling.shape, BF16), f32(SPLIT, NXY * PART, BLOCK)],
        [HBM, VMEM],
        [HBM] * 5,
        [
            pltpu.SMEM(mask.shape, jnp.int32),
            pltpu.VMEM(owner.shape, jnp.int32),
            pltpu.VMEM(own.shape, F32),
            pltpu.VMEM(coupling.shape, BF16),
            pltpu.VMEM(coupling.shape, BF16),
            DMA((4,)),
            DMA((coupling.shape[1] // TILE,)),
        ],
        PERMUTE_MIB,
        mask, owner, own, coupling, after,
    )


def reorder_kernel(owner_in, mine, other, after, mine_out, other_out, token, owner, terms, sem):
    copy = pltpu.make_async_copy(owner_in, owner, sem)
    copy.start()
    span, count = BLOCK // (NZ * PART), NZ * PART
    token[...] = jnp.zeros(token.shape, F32)
    left = lax.broadcasted_iota(jnp.int32, (BLOCK, BLOCK), 0)
    right = lax.broadcasted_iota(jnp.int32, (BLOCK, BLOCK), 1)

    def by_block(k):
        return (k // PART) % span * count + k // (span * PART) * PART + k % PART

    gather = (left == by_block(right)).astype(BF16)
    scatter = (right == by_block(left)).astype(F32)
    base = mine.shape[1] - NXY * PART
    for n, source in enumerate((mine, other)):
        for i in range(NXY // span):
            tile = source[:, base + 8 * i : base + 8 * (i + 1)].reshape(BLOCK, BLOCK)
            for m, term in enumerate(split3(tile)):
                moved = dot(gather, term).astype(BF16)
                for j in range(span):
                    row = (2 * m + n) * count
                    col = (span * i + j) * BLOCK
                    terms[row : row + count, col : col + BLOCK] = moved[j * count : (j + 1) * count]
    copy.wait()
    size = span * BLOCK
    for i in range(NXY // span):
        part = dot(terms[...], picks(owner, i, size))
        part = part[: 2 * count] + part[2 * count : 4 * count] + part[4 * count :]
        for n, out in enumerate((mine_out, other_out)):
            stack = jnp.concatenate(
                [part[n * count : (n + 1) * count, j * BLOCK : (j + 1) * BLOCK] for j in range(span)], axis=0
            )
            tile = jnp.dot(scatter, stack, precision=HIGHEST, preferred_element_type=F32)
            out[:, 8 * i : 8 * (i + 1)] = tile.reshape(NZ, 8, BLOCK)


def reorder(owner, mine, other, after):
    shape = (NZ, NXY * PART, BLOCK)
    return call(
        reorder_kernel,
        [f32(*shape)] * 2 + [f32(8, BLOCK)],
        [VMEM] * 3,
        [HBM, VMEM, VMEM, HBM],
        [pltpu.VMEM(owner.shape, jnp.int32), pltpu.VMEM((6 * NZ * PART, NXY * BLOCK), BF16), DMA],
        PERMUTE_MIB,
        owner, mine, other, after,
    )


def case_group(total, z):
    group = total.shape[0] * SPLIT // NZ
    first = z // SPLIT * group
    return total[first : first + group]


def pack_sum_kernel(parts, packed, out, buf, sem):
    group = parts.shape[1] * SPLIT // NZ
    total = -jnp.sum(parts[...], axis=0)
    for z in range(NZ):
        buf[z, :group] = case_group(total, z)
        buf[z, group:] = packed[z % SPLIT]
    copy = pltpu.make_async_copy(buf, out, sem)
    copy.start()
    copy.wait()


def sum_rows_kernel(parts, local_t, out):
    total = local_t[...] - jnp.sum(parts[...], axis=0)
    for z in range(NZ):
        out[z] = case_group(total, z)


def sum_cases_kernel(parts, out):
    total = jnp.sum(parts[:, : out.shape[1]], axis=0)
    out[...] = jnp.broadcast_to(total[None], out.shape)


def delta_kernel(core, rhs, mine, other, out):
    cases = rhs.shape[1]
    span = BLOCK // (NZ * PART)
    base = mine.shape[1] - NXY * PART
    acc_mine = jnp.zeros((span * cases, BLOCK), F32)
    acc_other = jnp.zeros((span * cases, BLOCK), F32)
    for i in range(NXY // span):
        left = rhs[span * i : span * (i + 1)].reshape(span * cases, BLOCK)
        rows = slice(base + 8 * i, base + 8 * (i + 1))
        acc_mine = acc_mine + rows_dot(left, mine[:, rows].reshape(BLOCK, BLOCK))
        acc_other = acc_other + rows_dot(left, other[:, rows].reshape(BLOCK, BLOCK))
    low = lax.broadcasted_iota(jnp.int32, (cases, BLOCK), 1) % 8 < PART

    def fold(acc):
        total = acc[:cases]
        for j in range(1, span):
            total = total + pltpu.roll(acc[j * cases : (j + 1) * cases], BLOCK - PART * j, 1)
        return jnp.where(low, total, 0.0)

    own, far_rows = fold(acc_mine), fold(acc_other)
    first = core[0] == 0
    total = jnp.where(first, own, far_rows) + pltpu.roll(jnp.where(first, far_rows, own), OWN, 1)
    half = cases // SPLIT
    tile = total[:half] + pltpu.roll(total[half:], PART, 1)
    out[...] = jnp.broadcast_to(tile[None], out.shape)


def rows_dot(left, rows):
    return lax.dot_general(
        left, rows, (((1,), (1,)), ((), ())), precision=HIGHEST, preferred_element_type=F32
    )


def spread_kernel(parts, out, cases_buf, buf, sems):
    half = parts.shape[1]
    low = lax.broadcasted_iota(jnp.int32, (half, BLOCK), 1) % (2 * PART) < PART
    for i in range(NZ // SPLIT):
        even, odd = parts[SPLIT * i], parts[SPLIT * i + 1]
        cases_buf[2 * half * i : 2 * half * i + half] = jnp.where(low, even, pltpu.roll(odd, PART, 1))
        cases_buf[2 * half * i + half : 2 * half * (i + 1)] = jnp.where(low, pltpu.roll(even, BLOCK - PART, 1), odd)
    buf[...] = cases_buf[...].T
    copies = [pltpu.make_async_copy(buf, out.at[i], sems.at[i]) for i in range(NXY)]
    for copy in copies:
        copy.start()
    for copy in copies:
        copy.wait()


def near_kernel(columns, after, out, sem):
    copy = pltpu.make_async_copy(columns.at[:, : out.shape[1]], out, sem)
    copy.start()
    copy.wait()


def near(columns, after):
    width, sep_width = columns.shape
    half = jax.ShapeDtypeStruct((width, sep_width // 2), BF16)
    return call(near_kernel, half, VMEM, [HBM] * 2, [DMA], 4, columns, after)


def coupled_product(low, high, delta):
    half = low.shape[1]
    return dot(low[...], delta[:half, :].astype(BF16)), lambda: dot(high[...], delta[half:, :].astype(BF16))


def own_rows(first, delta, count):
    return delta[pl.ds(pl.multiple_of(first[0], 8), count), :]


def middle_kernel(
    first, delta, cubic, low, after, columns_in, inverse_in, solved_in, matrix_in, load_in, state_out, contrib, sep_out,
    high, inverse, solved, matrix, load, mixed, part_buf, in_sems, out_sem, part_sems,
):
    half = low.shape[1]
    waits = fetch(
        (columns_in.at[:, half:], inverse_in, solved_in, matrix_in, load_in),
        (high, inverse, solved, matrix, load),
        in_sems,
    )
    sep_out[...] = own_rows(first, delta, sep_out.shape[0])
    coupled, rest = coupled_product(low, high, delta)
    waits[0].wait()
    coupled = coupled + rest()
    waits[1].wait()
    waits[2].wait()
    state = solved[...] - dot(inverse[...], coupled.astype(BF16))
    waits[3].wait()
    waits[4].wait()
    resid = load[...] - dot(matrix[...], state.astype(BF16)) - coupled
    resid = resid - cubic[...] * state * state * state
    mixed[...] = state + dot(inverse[...], resid.astype(BF16))
    copies = [pltpu.make_async_copy(mixed, state_out, out_sem)]
    copies[0].start()
    mixed_t = mixed[...].T.astype(BF16)
    count = part_sems.shape[0]
    size = 2 * half // count
    for i in range(count):
        source, at = (low, i) if i < count // 2 else (high, i - count // 2)
        part = dot(mixed_t, source[:, at * size : (at + 1) * size])
        copies.append(send_tile(part, i, part_buf, contrib, part_sems))
    for copy in copies:
        copy.wait()


def end_kernel(
    first, delta, low, sep_in, columns_in, inverse_in, mixed_in, out, sep_out,
    high, inverse, mixed, state, in_sems, out_sems,
):
    waits = fetch((columns_in.at[:, low.shape[1] :], inverse_in, mixed_in), (high, inverse, mixed), in_sems)
    sep_out[...] = sep_in[...] + own_rows(first, delta, sep_out.shape[0])
    back, rest = coupled_product(low, high, delta)
    waits[0].wait()
    back = (back + rest()).astype(BF16)
    waits[1].wait()
    waits[2].wait()
    count = out_sems.shape[0]
    rows = state.shape[0] // count
    copies = []
    for i in range(count):
        part = pl.ds(i * rows, rows)
        state[part, :] = mixed[part, :] - dot(inverse[part, :], back)
        copy = pltpu.make_async_copy(state.at[part], out.at[part], out_sems.at[i])
        copy.start()
        copies.append(copy)
    for copy in copies:
        copy.wait()


def exchange(parts, axes):
    return lax.all_to_all(parts, axes, 0, 0, tiled=True)


def correction(contrib, local, place, core, packed, rows, owner, columns):
    cases = contrib.shape[1]
    group = cases * SPLIT // NZ
    parts = exchange(contrib, ("x", "y"))
    first = rows is None
    if first:
        sent = (NZ, group + packed.shape[1], BLOCK)
        parts = call(pack_sum_kernel, far(sent), HBM, [VMEM] * 2, [pltpu.VMEM(sent, F32), DMA], 8, parts, packed)
    else:
        local_t = lax.dynamic_update_slice_in_dim(jnp.zeros((BLOCK, cases), F32), local, place, 0).T
        parts = call(sum_rows_kernel, f32(NZ, group, BLOCK), VMEM, [VMEM] * 2, [], 8, parts, local_t)
    parts = exchange(parts, "z")
    rhs = call(sum_cases_kernel, f32(NXY, group, BLOCK), VMEM, [VMEM], [], 4, parts)
    if first:
        parts, rhs = lax.optimization_barrier((parts, rhs))
        rows = (parts, lax.ppermute(parts, "c", [(0, 1), (1, 0)]))
    rhs = exchange(rhs, ("x", "y"))
    delta = call(
        delta_kernel, f32(NZ, group // SPLIT, BLOCK), VMEM, [SMEM] + [VMEM] * 3, [], 8, core, rhs, *rows
    )
    delta = exchange(delta, "z")
    delta = call(
        spread_kernel,
        far((NXY, BLOCK, cases)),
        HBM,
        [VMEM],
        [pltpu.VMEM((cases, BLOCK), F32), pltpu.VMEM((BLOCK, cases), F32), DMA((NXY,))],
        4,
        delta,
    )
    low = near(columns, delta)
    if first:
        rows = list(reorder(owner, *rows, delta))
    return exchange(delta, ("x", "y")).reshape(NXY * BLOCK, cases), rows, low


def on_device(
    leaf_matrix,
    leaf_inverse,
    coupling,
    cubic_coeff,
    leaf_load,
    sep_load,
    sep_matrix,
    sep_inverse,
    owner_map,
    block_mask,
):
    owned, cases = sep_load.shape
    width, sep_width = coupling.shape
    matrix_rows = lax.all_gather(sep_matrix, "c", axis=0, tiled=True)
    core = lax.axis_index("c").astype(jnp.int32)[None]
    place = lax.axis_index("z") * owned
    first = (lax.axis_index(("x", "y", "z")) * owned).astype(jnp.int32)[None]
    owner = owner_map[None, :]
    solved, contrib = start(first, block_mask, leaf_inverse, coupling, leaf_load, owner, sep_load)
    columns, packed = permute(block_mask, owner, sep_inverse, coupling, solved)

    delta, rows, low = correction(contrib, None, place, core, packed, None, owner, columns)
    local = sep_load - jnp.dot(matrix_rows, delta, precision=HIGHEST, preferred_element_type=F32)
    high = pltpu.VMEM((width, sep_width // 2), BF16)
    square = pltpu.VMEM(leaf_matrix.shape, BF16)
    state = pltpu.VMEM((width, cases), F32)
    mixed, contrib, sep_rows = call(
        middle_kernel,
        [far((width, cases)), far((NXY, cases, BLOCK)), f32(owned, cases)],
        [HBM, HBM, VMEM],
        [SMEM] + [VMEM] * 4 + [HBM] * 5,
        [high, square, state, square, state, state, pltpu.VMEM((NXY, cases, BLOCK), F32)]
        + [DMA((5,)), DMA, DMA((OUT_TILES,))],
        MIDDLE_MIB,
        first, delta, cubic_coeff[:, None], low, rows.pop(), columns, leaf_inverse, solved, leaf_matrix, leaf_load,
    )
    delta, rows, low = correction(contrib, local, place, core, None, rows, owner, columns)
    return call(
        end_kernel,
        [far((width, cases)), f32(owned, cases)],
        [HBM, VMEM],
        [SMEM] + [VMEM] * 3 + [HBM] * 3,
        [high, square, state, state, DMA((3,)), DMA((2,))],
        MIDDLE_MIB,
        first, delta, low, sep_rows, columns, leaf_inverse, mixed,
    )


def solution(mesh):
    grid = Mesh(mesh.devices.reshape(NX, NY, NZ, NC), ("x", "y", "z", "c"))
    leaf = ("x", "y", "z")
    in_specs = (
        P(leaf, None),
        P(leaf, None),
        P(leaf, None),
        P(leaf),
        P(leaf, "c"),
        P(leaf, "c"),
        P(leaf + ("c",), None),
        P(leaf + ("c",), None),
        P(),
        P(leaf, None),
    )
    out_specs = (P(leaf, "c"), P(leaf, "c"))
    return jax.shard_map(on_device, mesh=grid, in_specs=in_specs, out_specs=out_specs, check_vma=False)
```

```python
import jax
import jax.numpy as jnp
from jax import lax
from jax.experimental import pallas as pl
from jax.experimental.pallas import tpu as pltpu
from jax.sharding import Mesh, PartitionSpec as P

BLOCK = 128
NX, NY, NZ, NC = 4, 4, 16, 2
NXY = NX * NY
OWN = 4
SPLIT = 2
PART = OWN // SPLIT
TILE = 512
OUT_TILES = 4
START_MIB = 16
PERMUTE_MIB = 32
MIDDLE_MIB = 14
F32 = jnp.float32
BF16 = jnp.bfloat16
HIGHEST = lax.Precision.HIGHEST
MIB = 1024 * 1024
HBM = pl.BlockSpec(memory_space=pltpu.HBM)
SMEM = pl.BlockSpec(memory_space=pltpu.SMEM)
VMEM = pl.BlockSpec(memory_space=pltpu.VMEM)
DMA = pltpu.SemaphoreType.DMA


def dot(left, right):
    return jnp.dot(left, right, preferred_element_type=F32)


def f32(*shape):
    return jax.ShapeDtypeStruct(shape, F32)


def far(shape, dtype=F32):
    return pltpu.HBM(shape, dtype)


def call(kernel, out_shape, out_specs, in_specs, scratch, limit, *args):
    args = [pltpu.with_memory_space_constraint(x, pltpu.HBM) if spec is HBM else x for spec, x in zip(in_specs, args)]
    return pl.pallas_call(
        kernel,
        out_shape=out_shape,
        out_specs=out_specs,
        in_specs=in_specs,
        scratch_shapes=scratch,
        compiler_params=pltpu.CompilerParams(vmem_limit_bytes=limit * MIB),
    )(*args)


def fetch(sources, targets, sems):
    copies = [pltpu.make_async_copy(s, t, sems.at[i]) for i, (s, t) in enumerate(zip(sources, targets))]
    for copy in copies:
        copy.start()
    return copies


def send_tile(part, tile, scratch, contrib, sems):
    count = part.shape[1] // BLOCK
    first = tile * count
    for i in range(count):
        scratch[first + i] = part[:, i * BLOCK : (i + 1) * BLOCK]
    rows = pl.ds(first, count)
    copy = pltpu.make_async_copy(scratch.at[rows], contrib.at[rows], sems.at[tile])
    copy.start()
    return copy


def masked(mask, coupling):
    for i in range(coupling.shape[1] // BLOCK):
        cols = slice(i * BLOCK, (i + 1) * BLOCK)
        coupling[:, cols] = jnp.where(mask[0, i] != 0, coupling[:, cols], jnp.zeros((), BF16))


def picks(owner, tile, size):
    rows = lax.broadcasted_iota(jnp.int32, (owner.shape[1], size), 0)
    return (rows == owner[:, tile * size : (tile + 1) * size]).astype(BF16)


def split3(x):
    high = x.astype(BF16)
    rest = x - high.astype(F32)
    mid = rest.astype(BF16)
    return [high, mid, (rest - mid.astype(F32)).astype(BF16)]


def join(terms):
    return jnp.concatenate([x.astype(F32) for x in terms], axis=0).astype(BF16)


def start_kernel(
    first, mask_in, inverse_in, load_in, owner_in, sep_in, coupling_in, solved_out, contrib,
    mask, inverse, load, owner, sep, coupling, solved, part_buf, in_sems, out_sem, part_sems,
):
    waits = fetch(
        (mask_in, inverse_in, load_in, owner_in, sep_in, coupling_in),
        (mask, inverse, load, owner, sep, coupling),
        in_sems,
    )
    for wait in waits[1:3]:
        wait.wait()
    solved[...] = dot(inverse[...], load[...].astype(BF16))
    copies = [pltpu.make_async_copy(solved, solved_out, out_sem)]
    copies[0].start()
    mixed_t = solved[...].T.astype(BF16)
    for wait in waits[:1] + waits[3:]:
        wait.wait()
    own, sep_width = sep.shape[0], coupling.shape[1]
    loads_in = join(split3(sep[...]))
    size = sep_width // part_sems.shape[0]
    index = lax.broadcasted_iota(jnp.int32, (own, size), 0)
    target = jnp.zeros((own, size), jnp.int32)
    for j in range(own):
        target = jnp.where(index == j, owner[0, first[0] + j], target)
    for tile in range(part_sems.shape[0]):
        lanes = lax.broadcasted_iota(jnp.int32, (own, size), 1) + tile * size
        place = (lanes == target).astype(F32)
        loads = lax.dot_general(
            loads_in, join([place] * 3), (((0,), (0,)), ((), ())), preferred_element_type=F32
        )
        part = dot(mixed_t, coupling[:, tile * size : (tile + 1) * size])
        count = size // BLOCK
        kept = [
            jnp.where(mask[0, tile * count + i] != 0, part[:, i * BLOCK : (i + 1) * BLOCK], 0.0) for i in range(count)
        ]
        part = jnp.concatenate(kept, axis=1) - loads
        copies.append(send_tile(part, tile, part_buf, contrib, part_sems))
    for copy in copies:
        copy.wait()


def start(first, mask, inverse, coupling, load, owner, sep):
    cases = load.shape[1]
    return call(
        start_kernel,
        [far(load.shape), far((NXY, cases, BLOCK))],
        [HBM] * 2,
        [SMEM] + [HBM] * 6,
        [
            pltpu.SMEM(mask.shape, jnp.int32),
            pltpu.VMEM(inverse.shape, BF16),
            pltpu.VMEM(load.shape, F32),
            pltpu.SMEM(owner.shape, jnp.int32),
            pltpu.VMEM(sep.shape, F32),
            pltpu.VMEM(coupling.shape, BF16),
            pltpu.VMEM(load.shape, F32),
            pltpu.VMEM((NXY, cases, BLOCK), F32),
            DMA((6,)),
            DMA,
            DMA((OUT_TILES,)),
        ],
        START_MIB,
        first, mask, inverse, load, owner, sep, coupling,
    )


def permute_kernel(
    mask_in, owner_in, own_in, coupling_in, after, columns_out, packed,
    mask, owner, own, coupling, columns, in_sems, out_sems,
):
    waits = fetch((mask_in, owner_in, own_in, coupling_in), (mask, owner, own, coupling), in_sems)
    for wait in waits:
        wait.wait()
    masked(mask, coupling)
    terms = join(split3(own[...]))
    rows = jnp.zeros((3 * OWN, owner.shape[1]), F32)
    copies = []
    for tile in range(coupling.shape[1] // TILE):
        cols = pl.ds(tile * TILE, TILE)
        pick = picks(owner, tile, TILE)
        columns[:, cols] = dot(coupling[...], pick).astype(BF16)
        copy = pltpu.make_async_copy(columns.at[:, cols], columns_out.at[:, cols], out_sems.at[tile])
        copy.start()
        copies.append(copy)
        rows = rows + lax.dot_general(
            terms[:, tile * TILE : (tile + 1) * TILE], pick, (((1,), (1,)), ((), ())), preferred_element_type=F32
        )
    rows = rows[:OWN] + rows[OWN : 2 * OWN] + rows[2 * OWN :]
    for k in range(SPLIT):
        for t in range(NXY):
            packed[k, t * PART : (t + 1) * PART] = rows[k * PART : (k + 1) * PART, t * BLOCK : (t + 1) * BLOCK]
    for copy in copies:
        copy.wait()


def permute(mask, owner, own, coupling, after):
    return call(
        permute_kernel,
        [far(coupling.shape, BF16), f32(SPLIT, NXY * PART, BLOCK)],
        [HBM, VMEM],
        [HBM] * 5,
        [
            pltpu.SMEM(mask.shape, jnp.int32),
            pltpu.VMEM(owner.shape, jnp.int32),
            pltpu.VMEM(own.shape, F32),
            pltpu.VMEM(coupling.shape, BF16),
            pltpu.VMEM(coupling.shape, BF16),
            DMA((4,)),
            DMA((coupling.shape[1] // TILE,)),
        ],
        PERMUTE_MIB,
        mask, owner, own, coupling, after,
    )


def reorder_kernel(owner_in, mine, other, after, mine_out, other_out, token, owner, terms, sem):
    copy = pltpu.make_async_copy(owner_in, owner, sem)
    copy.start()
    span, count = BLOCK // (NZ * PART), NZ * PART
    token[...] = jnp.zeros(token.shape, F32)
    left = lax.broadcasted_iota(jnp.int32, (BLOCK, BLOCK), 0)
    right = lax.broadcasted_iota(jnp.int32, (BLOCK, BLOCK), 1)

    def by_block(k):
        return (k // PART) % span * count + k // (span * PART) * PART + k % PART

    gather = (left == by_block(right)).astype(BF16)
    scatter = (right == by_block(left)).astype(F32)
    base = mine.shape[1] - NXY * PART
    for n, source in enumerate((mine, other)):
        for i in range(NXY // span):
            tile = source[:, base + 8 * i : base + 8 * (i + 1)].reshape(BLOCK, BLOCK)
            for m, term in enumerate(split3(tile)):
                moved = dot(gather, term).astype(BF16)
                for j in range(span):
                    row = (2 * m + n) * count
                    col = (span * i + j) * BLOCK
                    terms[row : row + count, col : col + BLOCK] = moved[j * count : (j + 1) * count]
    copy.wait()
    size = span * BLOCK
    for i in range(NXY // span):
        part = dot(terms[...], picks(owner, i, size))
        part = part[: 2 * count] + part[2 * count : 4 * count] + part[4 * count :]
        for n, out in enumerate((mine_out, other_out)):
            stack = jnp.concatenate(
                [part[n * count : (n + 1) * count, j * BLOCK : (j + 1) * BLOCK] for j in range(span)], axis=0
            )
            tile = jnp.dot(scatter, stack, precision=HIGHEST, preferred_element_type=F32)
            out[:, 8 * i : 8 * (i + 1)] = tile.reshape(NZ, 8, BLOCK)


def reorder(owner, mine, other, after):
    shape = (NZ, NXY * PART, BLOCK)
    return call(
        reorder_kernel,
        [f32(*shape)] * 2 + [f32(8, BLOCK)],
        [VMEM] * 3,
        [HBM, VMEM, VMEM, HBM],
        [pltpu.VMEM(owner.shape, jnp.int32), pltpu.VMEM((6 * NZ * PART, NXY * BLOCK), BF16), DMA],
        PERMUTE_MIB,
        owner, mine, other, after,
    )


def case_group(total, z):
    group = total.shape[0] * SPLIT // NZ
    first = z // SPLIT * group
    return total[first : first + group]


def pack_sum_kernel(parts, packed, out):
    group = parts.shape[1] * SPLIT // NZ
    total = -jnp.sum(parts[...], axis=0)
    for z in range(NZ):
        out[z, :group] = case_group(total, z)
        out[z, group:] = packed[z % SPLIT]


def sum_rows_kernel(parts, local_t, out):
    total = local_t[...] - jnp.sum(parts[...], axis=0)
    for z in range(NZ):
        out[z] = case_group(total, z)


def sum_cases_kernel(parts, out):
    total = jnp.sum(parts[:, : out.shape[1]], axis=0)
    out[...] = jnp.broadcast_to(total[None], out.shape)


def delta_kernel(core, rhs, mine, other, out):
    cases = rhs.shape[1]
    span = BLOCK // (NZ * PART)
    base = mine.shape[1] - NXY * PART
    acc_mine = jnp.zeros((span * cases, BLOCK), F32)
    acc_other = jnp.zeros((span * cases, BLOCK), F32)
    for i in range(NXY // span):
        left = split3(rhs[span * i : span * (i + 1)].reshape(span * cases, BLOCK))
        rows = slice(base + 8 * i, base + 8 * (i + 1))
        acc_mine = acc_mine + rows_dot(left, mine[:, rows].reshape(BLOCK, BLOCK))
        acc_other = acc_other + rows_dot(left, other[:, rows].reshape(BLOCK, BLOCK))
    low = lax.broadcasted_iota(jnp.int32, (cases, BLOCK), 1) % 8 < PART

    def fold(acc):
        total = acc[:cases]
        for j in range(1, span):
            total = total + pltpu.roll(acc[j * cases : (j + 1) * cases], BLOCK - PART * j, 1)
        return jnp.where(low, total, 0.0)

    own, far_rows = fold(acc_mine), fold(acc_other)
    first = core[0] == 0
    total = jnp.where(first, own, far_rows) + pltpu.roll(jnp.where(first, far_rows, own), OWN, 1)
    half = cases // SPLIT
    tile = total[:half] + pltpu.roll(total[half:], PART, 1)
    out[...] = jnp.broadcast_to(tile[None], out.shape)


def rows_dot(left, rows):
    count = left[0].shape[0]
    total = jnp.zeros((count, rows.shape[0]), F32)
    for i, term in enumerate(split3(rows)):
        part = lax.dot_general(
            jnp.concatenate(left[: 3 - i], axis=0), term, (((1,), (1,)), ((), ())), preferred_element_type=F32
        )
        for j in range(3 - i):
            total = total + part[j * count : (j + 1) * count]
    return total


def spread_kernel(parts, out, cases_buf, buf, sems):
    half = parts.shape[1]
    low = lax.broadcasted_iota(jnp.int32, (half, BLOCK), 1) % (2 * PART) < PART
    for i in range(NZ // SPLIT):
        even, odd = parts[SPLIT * i], parts[SPLIT * i + 1]
        cases_buf[2 * half * i : 2 * half * i + half] = jnp.where(low, even, pltpu.roll(odd, PART, 1))
        cases_buf[2 * half * i + half : 2 * half * (i + 1)] = jnp.where(low, pltpu.roll(even, BLOCK - PART, 1), odd)
    buf[...] = cases_buf[...].T
    copies = [pltpu.make_async_copy(buf, out.at[i], sems.at[i]) for i in range(NXY)]
    for copy in copies:
        copy.start()
    for copy in copies:
        copy.wait()


def near_kernel(columns, after, out, sem):
    copy = pltpu.make_async_copy(columns.at[:, : out.shape[1]], out, sem)
    copy.start()
    copy.wait()


def near(columns, count, after):
    out = jax.ShapeDtypeStruct((columns.shape[0], count), BF16)
    return call(near_kernel, out, VMEM, [HBM] * 2, [DMA], 4, columns, after)


def coupled_product(low, high, delta):
    half = low.shape[1]
    return dot(low[...], delta[:half, :].astype(BF16)), lambda: dot(high[...], delta[half:, :].astype(BF16))


def own_rows(first, delta, count):
    return delta[pl.ds(pl.multiple_of(first[0], 8), count), :]


def middle_kernel(
    first, delta, cubic, low, after, columns_in, inverse_in, solved_in, matrix_in, load_in, state_out, contrib, sep_out,
    high, inverse, solved, matrix, load, mixed, part_buf, in_sems, out_sem, part_sems,
):
    half = low.shape[1]
    waits = fetch(
        (columns_in.at[:, half:], inverse_in, solved_in, matrix_in, load_in),
        (high, inverse, solved, matrix, load),
        in_sems,
    )
    sep_out[...] = own_rows(first, delta, sep_out.shape[0])
    coupled, rest = coupled_product(low, high, delta)
    waits[0].wait()
    coupled = coupled + rest()
    waits[1].wait()
    waits[2].wait()
    state = solved[...] - dot(inverse[...], coupled.astype(BF16))
    waits[3].wait()
    waits[4].wait()
    resid = load[...] - dot(matrix[...], state.astype(BF16)) - coupled
    resid = resid - cubic[...] * state * state * state
    mixed[...] = state + dot(inverse[...], resid.astype(BF16))
    copies = [pltpu.make_async_copy(mixed, state_out, out_sem)]
    copies[0].start()
    mixed_t = mixed[...].T.astype(BF16)
    count = part_sems.shape[0]
    size = 2 * half // count
    for i in range(count):
        source, at = (low, i) if i < count // 2 else (high, i - count // 2)
        part = dot(mixed_t, source[:, at * size : (at + 1) * size])
        copies.append(send_tile(part, i, part_buf, contrib, part_sems))
    for copy in copies:
        copy.wait()


def end_kernel(
    first, delta, columns, sep_in, inverse_in, mixed_in, out, sep_out, inverse, mixed, state, in_sems, out_sems
):
    waits = fetch((inverse_in, mixed_in), (inverse, mixed), in_sems)
    sep_out[...] = sep_in[...] + own_rows(first, delta, sep_out.shape[0])
    back = dot(columns[...], delta[...].astype(BF16)).astype(BF16)
    for wait in waits:
        wait.wait()
    count = out_sems.shape[0]
    rows = state.shape[0] // count
    copies = []
    for i in range(count):
        part = pl.ds(i * rows, rows)
        state[part, :] = mixed[part, :] - dot(inverse[part, :], back)
        copy = pltpu.make_async_copy(state.at[part], out.at[part], out_sems.at[i])
        copy.start()
        copies.append(copy)
    for copy in copies:
        copy.wait()


def exchange(parts, axes):
    return lax.all_to_all(parts, axes, 0, 0, tiled=True)


def correction(contrib, local, place, core, packed, rows, owner, columns):
    cases = contrib.shape[1]
    group = cases * SPLIT // NZ
    parts = exchange(contrib, ("x", "y"))
    first = rows is None
    if first:
        sent = (NZ, group + packed.shape[1], BLOCK)
        parts = call(pack_sum_kernel, f32(*sent), VMEM, [VMEM] * 2, [], 8, parts, packed)
    else:
        local_t = lax.dynamic_update_slice_in_dim(jnp.zeros((BLOCK, cases), F32), local, place, 0).T
        parts = call(sum_rows_kernel, f32(NZ, group, BLOCK), VMEM, [VMEM] * 2, [], 8, parts, local_t)
    parts = exchange(parts, "z")
    rhs = call(sum_cases_kernel, f32(NXY, group, BLOCK), VMEM, [VMEM], [], 4, parts)
    if first:
        parts, rhs = lax.optimization_barrier((parts, rhs))
        rows = (parts, lax.ppermute(parts, "c", [(0, 1), (1, 0)]))
    rhs = exchange(rhs, ("x", "y"))
    delta = call(
        delta_kernel, f32(NZ, group // SPLIT, BLOCK), VMEM, [SMEM] + [VMEM] * 3, [], 8, core, rhs, *rows
    )
    delta = exchange(delta, "z")
    delta = call(
        spread_kernel,
        far((NXY, BLOCK, cases)),
        HBM,
        [VMEM],
        [pltpu.VMEM((cases, BLOCK), F32), pltpu.VMEM((BLOCK, cases), F32), DMA((NXY,))],
        4,
        delta,
    )
    low = near(columns, columns.shape[1] // (2 if first else 1), delta)
    if first:
        rows = list(reorder(owner, *rows, delta))
    return exchange(delta, ("x", "y")).reshape(NXY * BLOCK, cases), rows, low


def on_device(
    leaf_matrix,
    leaf_inverse,
    coupling,
    cubic_coeff,
    leaf_load,
    sep_load,
    sep_matrix,
    sep_inverse,
    owner_map,
    block_mask,
):
    owned, cases = sep_load.shape
    width, sep_width = coupling.shape
    matrix_rows = lax.all_gather(sep_matrix, "c", axis=0, tiled=True)
    core = lax.axis_index("c").astype(jnp.int32)[None]
    place = lax.axis_index("z") * owned
    first = (lax.axis_index(("x", "y", "z")) * owned).astype(jnp.int32)[None]
    owner = owner_map[None, :]
    solved, contrib = start(first, block_mask, leaf_inverse, coupling, leaf_load, owner, sep_load)
    columns, packed = permute(block_mask, owner, sep_inverse, coupling, solved)

    delta, rows, low = correction(contrib, None, place, core, packed, None, owner, columns)
    local = sep_load - jnp.dot(matrix_rows, delta, precision=HIGHEST, preferred_element_type=F32)
    high = pltpu.VMEM((width, sep_width // 2), BF16)
    square = pltpu.VMEM(leaf_matrix.shape, BF16)
    state = pltpu.VMEM((width, cases), F32)
    mixed, contrib, sep_rows = call(
        middle_kernel,
        [far((width, cases)), far((NXY, cases, BLOCK)), f32(owned, cases)],
        [HBM, HBM, VMEM],
        [SMEM] + [VMEM] * 4 + [HBM] * 5,
        [high, square, state, square, state, state, pltpu.VMEM((NXY, cases, BLOCK), F32)]
        + [DMA((5,)), DMA, DMA((OUT_TILES,))],
        MIDDLE_MIB,
        first, delta, cubic_coeff[:, None], low, rows.pop(), columns, leaf_inverse, solved, leaf_matrix, leaf_load,
    )
    delta, rows, low = correction(contrib, local, place, core, None, rows, owner, columns)
    return call(
        end_kernel,
        [far((width, cases)), f32(owned, cases)],
        [HBM, VMEM],
        [SMEM] + [VMEM] * 3 + [HBM] * 2,
        [square, state, state, DMA((2,)), DMA((2,))],
        MIDDLE_MIB,
        first, delta, low, sep_rows, leaf_inverse, mixed,
    )


def solution(mesh):
    grid = Mesh(mesh.devices.reshape(NX, NY, NZ, NC), ("x", "y", "z", "c"))
    leaf = ("x", "y", "z")
    in_specs = (
        P(leaf, None),
        P(leaf, None),
        P(leaf, None),
        P(leaf),
        P(leaf, "c"),
        P(leaf, "c"),
        P(leaf + ("c",), None),
        P(leaf + ("c",), None),
        P(),
        P(leaf, None),
    )
    out_specs = (P(leaf, "c"), P(leaf, "c"))
    return jax.shard_map(on_device, mesh=grid, in_specs=in_specs, out_specs=out_specs, check_vma=False)
```

```python
import jax
import jax.numpy as jnp
from jax import lax
from jax.experimental import pallas as pl
from jax.experimental.pallas import tpu as pltpu
from jax.sharding import Mesh, PartitionSpec as P

BLOCK = 128
NX, NY, NZ, NC = 4, 4, 16, 2
NXY = NX * NY
OWN = 4
SPLIT = 2
PART = OWN // SPLIT
TILE = 512
OUT_TILES = 4
START_MIB = 16
PERMUTE_MIB = 32
MIDDLE_MIB = 14
F32 = jnp.float32
BF16 = jnp.bfloat16
HIGHEST = lax.Precision.HIGHEST
MIB = 1024 * 1024
HBM = pl.BlockSpec(memory_space=pltpu.HBM)
SMEM = pl.BlockSpec(memory_space=pltpu.SMEM)
VMEM = pl.BlockSpec(memory_space=pltpu.VMEM)
DMA = pltpu.SemaphoreType.DMA


def dot(left, right):
    return jnp.dot(left, right, preferred_element_type=F32)


def f32(*shape):
    return jax.ShapeDtypeStruct(shape, F32)


def far(shape, dtype=F32):
    return pltpu.HBM(shape, dtype)


def call(kernel, out_shape, out_specs, in_specs, scratch, limit, *args):
    args = [pltpu.with_memory_space_constraint(x, pltpu.HBM) if spec is HBM else x for spec, x in zip(in_specs, args)]
    return pl.pallas_call(
        kernel,
        out_shape=out_shape,
        out_specs=out_specs,
        in_specs=in_specs,
        scratch_shapes=scratch,
        compiler_params=pltpu.CompilerParams(vmem_limit_bytes=limit * MIB),
    )(*args)


def fetch(sources, targets, sems):
    copies = [pltpu.make_async_copy(s, t, sems.at[i]) for i, (s, t) in enumerate(zip(sources, targets))]
    for copy in copies:
        copy.start()
    return copies


def send_tile(part, tile, scratch, contrib, sems):
    count = part.shape[1] // BLOCK
    first = tile * count
    for i in range(count):
        scratch[first + i] = part[:, i * BLOCK : (i + 1) * BLOCK]
    rows = pl.ds(first, count)
    copy = pltpu.make_async_copy(scratch.at[rows], contrib.at[rows], sems.at[tile])
    copy.start()
    return copy


def masked(mask, coupling):
    for i in range(coupling.shape[1] // BLOCK):
        cols = slice(i * BLOCK, (i + 1) * BLOCK)
        coupling[:, cols] = jnp.where(mask[0, i] != 0, coupling[:, cols], jnp.zeros((), BF16))


def picks(owner, tile, size):
    rows = lax.broadcasted_iota(jnp.int32, (owner.shape[1], size), 0)
    return (rows == owner[:, tile * size : (tile + 1) * size]).astype(BF16)


def split3(x):
    high = x.astype(BF16)
    rest = x - high.astype(F32)
    mid = rest.astype(BF16)
    return [high, mid, (rest - mid.astype(F32)).astype(BF16)]


def join(terms):
    return jnp.concatenate([x.astype(F32) for x in terms], axis=0).astype(BF16)


def start_kernel(
    first, mask_in, inverse_in, load_in, owner_in, sep_in, coupling_in, solved_out, contrib,
    mask, inverse, load, owner, sep, coupling, solved, part_buf, in_sems, out_sem, part_sems,
):
    waits = fetch(
        (mask_in, inverse_in, load_in, owner_in, sep_in, coupling_in),
        (mask, inverse, load, owner, sep, coupling),
        in_sems,
    )
    for wait in waits[1:3]:
        wait.wait()
    solved[...] = dot(inverse[...], load[...].astype(BF16))
    copies = [pltpu.make_async_copy(solved, solved_out, out_sem)]
    copies[0].start()
    mixed_t = solved[...].T.astype(BF16)
    for wait in waits[:1] + waits[3:]:
        wait.wait()
    own, sep_width = sep.shape[0], coupling.shape[1]
    loads_in = join(split3(sep[...]))
    size = sep_width // part_sems.shape[0]
    index = lax.broadcasted_iota(jnp.int32, (own, size), 0)
    target = jnp.zeros((own, size), jnp.int32)
    for j in range(own):
        target = jnp.where(index == j, owner[0, first[0] + j], target)
    for tile in range(part_sems.shape[0]):
        lanes = lax.broadcasted_iota(jnp.int32, (own, size), 1) + tile * size
        place = (lanes == target).astype(F32)
        loads = lax.dot_general(
            loads_in, join([place] * 3), (((0,), (0,)), ((), ())), preferred_element_type=F32
        )
        part = dot(mixed_t, coupling[:, tile * size : (tile + 1) * size])
        count = size // BLOCK
        kept = [
            jnp.where(mask[0, tile * count + i] != 0, part[:, i * BLOCK : (i + 1) * BLOCK], 0.0) for i in range(count)
        ]
        part = jnp.concatenate(kept, axis=1) - loads
        copies.append(send_tile(part, tile, part_buf, contrib, part_sems))
    for copy in copies:
        copy.wait()


def start(first, mask, inverse, coupling, load, owner, sep):
    cases = load.shape[1]
    return call(
        start_kernel,
        [far(load.shape), far((NXY, cases, BLOCK))],
        [HBM] * 2,
        [SMEM] + [HBM] * 6,
        [
            pltpu.SMEM(mask.shape, jnp.int32),
            pltpu.VMEM(inverse.shape, BF16),
            pltpu.VMEM(load.shape, F32),
            pltpu.SMEM(owner.shape, jnp.int32),
            pltpu.VMEM(sep.shape, F32),
            pltpu.VMEM(coupling.shape, BF16),
            pltpu.VMEM(load.shape, F32),
            pltpu.VMEM((NXY, cases, BLOCK), F32),
            DMA((6,)),
            DMA,
            DMA((OUT_TILES,)),
        ],
        START_MIB,
        first, mask, inverse, load, owner, sep, coupling,
    )


def permute_kernel(
    mask_in, owner_in, own_in, coupling_in, after, columns_out, columns_again, packed,
    mask, owner, own, coupling, columns, in_sems, out_sems,
):
    waits = fetch((mask_in, owner_in, own_in, coupling_in), (mask, owner, own, coupling), in_sems)
    for wait in waits:
        wait.wait()
    masked(mask, coupling)
    terms = join(split3(own[...]))
    rows = jnp.zeros((3 * OWN, owner.shape[1]), F32)
    copies = []
    for tile in range(coupling.shape[1] // TILE):
        cols = pl.ds(tile * TILE, TILE)
        pick = picks(owner, tile, TILE)
        columns[:, cols] = dot(coupling[...], pick).astype(BF16)
        for i, out in enumerate((columns_out, columns_again)):
            copy = pltpu.make_async_copy(columns.at[:, cols], out.at[:, cols], out_sems.at[i, tile])
            copy.start()
            copies.append(copy)
        rows = rows + lax.dot_general(
            terms[:, tile * TILE : (tile + 1) * TILE], pick, (((1,), (1,)), ((), ())), preferred_element_type=F32
        )
    rows = rows[:OWN] + rows[OWN : 2 * OWN] + rows[2 * OWN :]
    for k in range(SPLIT):
        for t in range(NXY):
            packed[k, t * PART : (t + 1) * PART] = rows[k * PART : (k + 1) * PART, t * BLOCK : (t + 1) * BLOCK]
    for copy in copies:
        copy.wait()


def permute(mask, owner, own, coupling, after):
    return call(
        permute_kernel,
        [far(coupling.shape, BF16)] * 2 + [f32(SPLIT, NXY * PART, BLOCK)],
        [HBM, HBM, VMEM],
        [HBM] * 5,
        [
            pltpu.SMEM(mask.shape, jnp.int32),
            pltpu.VMEM(owner.shape, jnp.int32),
            pltpu.VMEM(own.shape, F32),
            pltpu.VMEM(coupling.shape, BF16),
            pltpu.VMEM(coupling.shape, BF16),
            DMA((4,)),
            DMA((2, coupling.shape[1] // TILE)),
        ],
        PERMUTE_MIB,
        mask, owner, own, coupling, after,
    )


def reorder_kernel(owner_in, mine, other, after, mine_out, other_out, token, owner, terms, sem):
    copy = pltpu.make_async_copy(owner_in, owner, sem)
    copy.start()
    span, count = BLOCK // (NZ * PART), NZ * PART
    token[...] = jnp.zeros(token.shape, F32)
    left = lax.broadcasted_iota(jnp.int32, (BLOCK, BLOCK), 0)
    right = lax.broadcasted_iota(jnp.int32, (BLOCK, BLOCK), 1)

    def by_block(k):
        return (k // PART) % span * count + k // (span * PART) * PART + k % PART

    gather = (left == by_block(right)).astype(BF16)
    scatter = (right == by_block(left)).astype(F32)
    base = mine.shape[1] - NXY * PART
    for n, source in enumerate((mine, other)):
        for i in range(NXY // span):
            tile = source[:, base + 8 * i : base + 8 * (i + 1)].reshape(BLOCK, BLOCK)
            for m, term in enumerate(split3(tile)):
                moved = dot(gather, term).astype(BF16)
                for j in range(span):
                    row = (2 * m + n) * count
                    col = (span * i + j) * BLOCK
                    terms[row : row + count, col : col + BLOCK] = moved[j * count : (j + 1) * count]
    copy.wait()
    size = span * BLOCK
    for i in range(NXY // span):
        part = dot(terms[...], picks(owner, i, size))
        part = part[: 2 * count] + part[2 * count : 4 * count] + part[4 * count :]
        for n, out in enumerate((mine_out, other_out)):
            stack = jnp.concatenate(
                [part[n * count : (n + 1) * count, j * BLOCK : (j + 1) * BLOCK] for j in range(span)], axis=0
            )
            tile = jnp.dot(scatter, stack, precision=HIGHEST, preferred_element_type=F32)
            out[:, 8 * i : 8 * (i + 1)] = tile.reshape(NZ, 8, BLOCK)


def reorder(owner, mine, other, after):
    shape = (NZ, NXY * PART, BLOCK)
    return call(
        reorder_kernel,
        [f32(*shape)] * 2 + [f32(8, BLOCK)],
        [VMEM] * 3,
        [HBM, VMEM, VMEM, HBM],
        [pltpu.VMEM(owner.shape, jnp.int32), pltpu.VMEM((6 * NZ * PART, NXY * BLOCK), BF16), DMA],
        PERMUTE_MIB,
        owner, mine, other, after,
    )


def case_group(total, z):
    group = total.shape[0] * SPLIT // NZ
    first = z // SPLIT * group
    return total[first : first + group]


def pack_sum_kernel(parts, packed, out):
    group = parts.shape[1] * SPLIT // NZ
    total = -jnp.sum(parts[...], axis=0)
    for z in range(NZ):
        out[z, :group] = case_group(total, z)
        out[z, group:] = packed[z % SPLIT]


def sum_rows_kernel(parts, local_t, after, out):
    total = local_t[...] - jnp.sum(parts[...], axis=0)
    for z in range(NZ):
        out[z] = case_group(total, z)


def sum_cases_kernel(parts, out):
    total = jnp.sum(parts[:, : out.shape[1]], axis=0)
    out[...] = jnp.broadcast_to(total[None], out.shape)


def delta_kernel(core, rhs, mine, other, out):
    cases = rhs.shape[1]
    span = BLOCK // (NZ * PART)
    base = mine.shape[1] - NXY * PART
    acc_mine = jnp.zeros((span * cases, BLOCK), F32)
    acc_other = jnp.zeros((span * cases, BLOCK), F32)
    for i in range(NXY // span):
        left = split3(rhs[span * i : span * (i + 1)].reshape(span * cases, BLOCK))
        rows = slice(base + 8 * i, base + 8 * (i + 1))
        acc_mine = acc_mine + rows_dot(left, mine[:, rows].reshape(BLOCK, BLOCK))
        acc_other = acc_other + rows_dot(left, other[:, rows].reshape(BLOCK, BLOCK))
    low = lax.broadcasted_iota(jnp.int32, (cases, BLOCK), 1) % 8 < PART

    def fold(acc):
        total = acc[:cases]
        for j in range(1, span):
            total = total + pltpu.roll(acc[j * cases : (j + 1) * cases], BLOCK - PART * j, 1)
        return jnp.where(low, total, 0.0)

    own, far_rows = fold(acc_mine), fold(acc_other)
    first = core[0] == 0
    total = jnp.where(first, own, far_rows) + pltpu.roll(jnp.where(first, far_rows, own), OWN, 1)
    half = cases // SPLIT
    tile = total[:half] + pltpu.roll(total[half:], PART, 1)
    out[...] = jnp.broadcast_to(tile[None], out.shape)


def rows_dot(left, rows):
    count = left[0].shape[0]
    total = jnp.zeros((count, rows.shape[0]), F32)
    for i, term in enumerate(split3(rows)):
        part = lax.dot_general(
            jnp.concatenate(left[: 3 - i], axis=0), term, (((1,), (1,)), ((), ())), preferred_element_type=F32
        )
        for j in range(3 - i):
            total = total + part[j * count : (j + 1) * count]
    return total


def unpacked(parts, cases_buf):
    half = parts.shape[1]
    low = lax.broadcasted_iota(jnp.int32, (half, BLOCK), 1) % (2 * PART) < PART
    for i in range(NZ // SPLIT):
        even, odd = parts[SPLIT * i], parts[SPLIT * i + 1]
        cases_buf[2 * half * i : 2 * half * i + half] = jnp.where(low, even, pltpu.roll(odd, PART, 1))
        cases_buf[2 * half * i + half : 2 * half * (i + 1)] = jnp.where(low, pltpu.roll(even, BLOCK - PART, 1), odd)
    return cases_buf[...].T


def spread_kernel(parts, out, cases_buf):
    out[...] = jnp.broadcast_to(unpacked(parts, cases_buf)[None], out.shape)


def own_rows(first, delta, count):
    return delta[pl.ds(pl.multiple_of(first[0], 8), count), :]


def middle_kernel(
    first, delta, cubic_row, columns, inverse, solved, matrix, load, mixed_out, contrib, sep_out,
    mixed, part_buf, mixed_sem, part_sems,
):
    sep_out[...] = own_rows(first, delta, sep_out.shape[0])
    cubic = jnp.broadcast_to(cubic_row[...], (8, cubic_row.shape[1])).T[:, :1]
    coupled = dot(columns[...], delta[...].astype(BF16))
    state = solved[...] - dot(inverse[...], coupled.astype(BF16))
    resid = load[...] - dot(matrix[...], state.astype(BF16)) - coupled
    resid = resid - cubic * state * state * state
    mixed[...] = state + dot(inverse[...], resid.astype(BF16))
    mixed_t = mixed[...].T.astype(BF16)
    count = part_sems.shape[0]
    size = columns.shape[1] // count
    copies = [pltpu.make_async_copy(mixed, mixed_out, mixed_sem)]
    copies[0].start()
    for i in range(count):
        part = dot(mixed_t, columns[:, i * size : (i + 1) * size])
        copies.append(send_tile(part, i, part_buf, contrib, part_sems))
    for copy in copies:
        copy.wait()


def end_kernel(first, delta, sep_in, columns, inverse, mixed, out, sep_out, state, out_sems):
    sep_out[...] = sep_in[...] + own_rows(first, delta, sep_out.shape[0])
    back = dot(columns[...], delta[...].astype(BF16)).astype(BF16)
    count = out_sems.shape[0]
    rows = state.shape[0] // count
    copies = []
    for i in range(count):
        part = pl.ds(i * rows, rows)
        state[part, :] = mixed[part, :] - dot(inverse[part, :], back)
        copy = pltpu.make_async_copy(state.at[part], out.at[part], out_sems.at[i])
        copy.start()
        copies.append(copy)
    for copy in copies:
        copy.wait()


def exchange(parts, axes):
    return lax.all_to_all(parts, axes, 0, 0, tiled=True)


def correction(contrib, local, place, core, packed, rows, owner):
    cases = contrib.shape[1]
    group = cases * SPLIT // NZ
    parts = exchange(contrib, ("x", "y"))
    first = rows is None
    if first:
        sent = (NZ, group + packed.shape[1], BLOCK)
        parts = call(pack_sum_kernel, f32(*sent), VMEM, [VMEM] * 2, [], 8, parts, packed)
    else:
        local_t = lax.dynamic_update_slice_in_dim(jnp.zeros((BLOCK, cases), F32), local, place, 0).T
        *rows, token = reorder(owner, *rows, contrib)
        parts = call(sum_rows_kernel, f32(NZ, group, BLOCK), VMEM, [VMEM] * 3, [], 8, parts, local_t, token)
    parts = exchange(parts, "z")
    rhs = call(sum_cases_kernel, f32(NXY, group, BLOCK), VMEM, [VMEM], [], 4, parts)
    if first:
        parts, rhs = lax.optimization_barrier((parts, rhs))
        rows = (parts, lax.ppermute(parts, "c", [(0, 1), (1, 0)]))
    rhs = exchange(rhs, ("x", "y"))
    delta = call(
        delta_kernel, f32(NZ, group // SPLIT, BLOCK), VMEM, [SMEM] + [VMEM] * 3, [], 8, core, rhs, *rows
    )
    delta = exchange(delta, "z")
    delta = call(
        spread_kernel, f32(NXY, BLOCK, cases), VMEM, [VMEM], [pltpu.VMEM((cases, BLOCK), F32)], 4, delta
    )
    return exchange(delta, ("x", "y")).reshape(NXY * BLOCK, cases), rows


def on_device(
    leaf_matrix,
    leaf_inverse,
    coupling,
    cubic_coeff,
    leaf_load,
    sep_load,
    sep_matrix,
    sep_inverse,
    owner_map,
    block_mask,
):
    owned, cases = sep_load.shape
    width, sep_width = coupling.shape
    matrix_rows = lax.all_gather(sep_matrix, "c", axis=0, tiled=True)
    core = lax.axis_index("c").astype(jnp.int32)[None]
    place = lax.axis_index("z") * owned
    first = (lax.axis_index(("x", "y", "z")) * owned).astype(jnp.int32)[None]
    owner = owner_map[None, :]
    solved, contrib = start(first, block_mask, leaf_inverse, coupling, leaf_load, owner, sep_load)
    columns, columns_again, packed = permute(block_mask, owner, sep_inverse, coupling, solved)

    delta, rows = correction(contrib, None, place, core, packed, None, owner)
    local = sep_load - jnp.dot(matrix_rows, delta, precision=HIGHEST, preferred_element_type=F32)
    mixed, contrib, sep_rows = call(
        middle_kernel,
        [far((width, cases)), far((NXY, cases, BLOCK)), f32(owned, cases)],
        [HBM, HBM, VMEM],
        [SMEM] + [VMEM] * 7,
        [pltpu.VMEM((width, cases), F32), pltpu.VMEM((NXY, cases, BLOCK), F32), DMA, DMA((OUT_TILES,))],
        MIDDLE_MIB,
        first, delta, cubic_coeff[None, :], columns, leaf_inverse, solved, leaf_matrix, leaf_load,
    )
    delta, rows = correction(contrib, local, place, core, None, rows, owner)
    return call(
        end_kernel,
        [far((width, cases)), f32(owned, cases)],
        [HBM, VMEM],
        [SMEM] + [VMEM] * 5,
        [pltpu.VMEM((width, cases), F32), DMA((2,))],
        MIDDLE_MIB,
        first, delta, sep_rows, columns_again, leaf_inverse, mixed,
    )


def solution(mesh):
    grid = Mesh(mesh.devices.reshape(NX, NY, NZ, NC), ("x", "y", "z", "c"))
    leaf = ("x", "y", "z")
    in_specs = (
        P(leaf, None),
        P(leaf, None),
        P(leaf, None),
        P(leaf),
        P(leaf, "c"),
        P(leaf, "c"),
        P(leaf + ("c",), None),
        P(leaf + ("c",), None),
        P(),
        P(leaf, None),
    )
    out_specs = (P(leaf, "c"), P(leaf, "c"))
    return jax.shard_map(on_device, mesh=grid, in_specs=in_specs, out_specs=out_specs, check_vma=False)
```

```python
import jax
import jax.numpy as jnp
from jax import lax
from jax.experimental import pallas as pl
from jax.experimental.pallas import tpu as pltpu
from jax.sharding import Mesh, PartitionSpec as P

BLOCK = 128
NX, NY, NZ, NC = 4, 4, 16, 2
NXY = NX * NY
OWN = 4
SPLIT = 2
PART = OWN // SPLIT
TILE = 512
OUT_TILES = 4
START_MIB = 16
PERMUTE_MIB = 32
MIDDLE_MIB = 14
F32 = jnp.float32
BF16 = jnp.bfloat16
HIGHEST = lax.Precision.HIGHEST
MIB = 1024 * 1024
HBM = pl.BlockSpec(memory_space=pltpu.HBM)
SMEM = pl.BlockSpec(memory_space=pltpu.SMEM)
VMEM = pl.BlockSpec(memory_space=pltpu.VMEM)
DMA = pltpu.SemaphoreType.DMA


def dot(left, right):
    return jnp.dot(left, right, preferred_element_type=F32)


def f32(*shape):
    return jax.ShapeDtypeStruct(shape, F32)


def far(shape, dtype=F32):
    return pltpu.HBM(shape, dtype)


def call(kernel, out_shape, out_specs, in_specs, scratch, limit, *args):
    args = [pltpu.with_memory_space_constraint(x, pltpu.HBM) if spec is HBM else x for spec, x in zip(in_specs, args)]
    return pl.pallas_call(
        kernel,
        out_shape=out_shape,
        out_specs=out_specs,
        in_specs=in_specs,
        scratch_shapes=scratch,
        compiler_params=pltpu.CompilerParams(vmem_limit_bytes=limit * MIB),
    )(*args)


def fetch(sources, targets, sems):
    copies = [pltpu.make_async_copy(s, t, sems.at[i]) for i, (s, t) in enumerate(zip(sources, targets))]
    for copy in copies:
        copy.start()
    return copies


def send_tile(part, tile, scratch, contrib, sems):
    count = part.shape[1] // BLOCK
    first = tile * count
    for i in range(count):
        scratch[first + i] = part[:, i * BLOCK : (i + 1) * BLOCK]
    rows = pl.ds(first, count)
    copy = pltpu.make_async_copy(scratch.at[rows], contrib.at[rows], sems.at[tile])
    copy.start()
    return copy


def masked(mask, coupling):
    for i in range(coupling.shape[1] // BLOCK):
        cols = slice(i * BLOCK, (i + 1) * BLOCK)
        coupling[:, cols] = jnp.where(mask[0, i] != 0, coupling[:, cols], jnp.zeros((), BF16))


def picks(owner, tile, size):
    rows = lax.broadcasted_iota(jnp.int32, (owner.shape[1], size), 0)
    return (rows == owner[:, tile * size : (tile + 1) * size]).astype(BF16)


def split3(x):
    high = x.astype(BF16)
    rest = x - high.astype(F32)
    mid = rest.astype(BF16)
    return [high, mid, (rest - mid.astype(F32)).astype(BF16)]


def join(terms):
    return jnp.concatenate([x.astype(F32) for x in terms], axis=0).astype(BF16)


def start_kernel(
    first, mask_in, inverse_in, load_in, owner_in, sep_in, coupling_in, solved_out, contrib,
    mask, inverse, load, owner, sep, coupling, solved, part_buf, in_sems, out_sem, part_sems,
):
    waits = fetch(
        (mask_in, inverse_in, load_in, owner_in, sep_in, coupling_in),
        (mask, inverse, load, owner, sep, coupling),
        in_sems,
    )
    for wait in waits[1:3]:
        wait.wait()
    solved[...] = dot(inverse[...], load[...].astype(BF16))
    copies = [pltpu.make_async_copy(solved, solved_out, out_sem)]
    copies[0].start()
    mixed_t = solved[...].T.astype(BF16)
    for wait in waits[:1] + waits[3:]:
        wait.wait()
    own, sep_width = sep.shape[0], coupling.shape[1]
    loads_in = join(split3(sep[...]))
    size = sep_width // part_sems.shape[0]
    index = lax.broadcasted_iota(jnp.int32, (own, size), 0)
    target = jnp.zeros((own, size), jnp.int32)
    for j in range(own):
        target = jnp.where(index == j, owner[0, first[0] + j], target)
    for tile in range(part_sems.shape[0]):
        lanes = lax.broadcasted_iota(jnp.int32, (own, size), 1) + tile * size
        place = (lanes == target).astype(F32)
        loads = lax.dot_general(
            loads_in, join([place] * 3), (((0,), (0,)), ((), ())), preferred_element_type=F32
        )
        part = dot(mixed_t, coupling[:, tile * size : (tile + 1) * size])
        count = size // BLOCK
        kept = [
            jnp.where(mask[0, tile * count + i] != 0, part[:, i * BLOCK : (i + 1) * BLOCK], 0.0) for i in range(count)
        ]
        part = jnp.concatenate(kept, axis=1) - loads
        copies.append(send_tile(part, tile, part_buf, contrib, part_sems))
    for copy in copies:
        copy.wait()


def start(first, mask, inverse, coupling, load, owner, sep):
    cases = load.shape[1]
    return call(
        start_kernel,
        [far(load.shape), far((NXY, cases, BLOCK))],
        [HBM] * 2,
        [SMEM] + [HBM] * 6,
        [
            pltpu.SMEM(mask.shape, jnp.int32),
            pltpu.VMEM(inverse.shape, BF16),
            pltpu.VMEM(load.shape, F32),
            pltpu.SMEM(owner.shape, jnp.int32),
            pltpu.VMEM(sep.shape, F32),
            pltpu.VMEM(coupling.shape, BF16),
            pltpu.VMEM(load.shape, F32),
            pltpu.VMEM((NXY, cases, BLOCK), F32),
            DMA((6,)),
            DMA,
            DMA((OUT_TILES,)),
        ],
        START_MIB,
        first, mask, inverse, load, owner, sep, coupling,
    )


def permute_kernel(
    mask_in, owner_in, own_in, matrix_in, coupling_in, after, columns_out, columns_again, packed, matrix_rows,
    mask, owner, own, matrix, coupling, columns, in_sems, out_sems,
):
    waits = fetch(
        (mask_in, owner_in, own_in, matrix_in, coupling_in), (mask, owner, own, matrix, coupling), in_sems
    )
    for wait in waits:
        wait.wait()
    matrix_rows[...] = jnp.zeros(matrix_rows.shape, F32)
    for t in range(NXY):
        matrix_rows[t, :OWN] = matrix[:, t * BLOCK : (t + 1) * BLOCK]
    masked(mask, coupling)
    terms = join(split3(own[...]))
    rows = jnp.zeros((3 * OWN, owner.shape[1]), F32)
    copies = []
    for tile in range(coupling.shape[1] // TILE):
        cols = pl.ds(tile * TILE, TILE)
        pick = picks(owner, tile, TILE)
        columns[:, cols] = dot(coupling[...], pick).astype(BF16)
        for i, out in enumerate((columns_out, columns_again)):
            copy = pltpu.make_async_copy(columns.at[:, cols], out.at[:, cols], out_sems.at[i, tile])
            copy.start()
            copies.append(copy)
        rows = rows + lax.dot_general(
            terms[:, tile * TILE : (tile + 1) * TILE], pick, (((1,), (1,)), ((), ())), preferred_element_type=F32
        )
    rows = rows[:OWN] + rows[OWN : 2 * OWN] + rows[2 * OWN :]
    for k in range(SPLIT):
        for t in range(NXY):
            packed[k, t * PART : (t + 1) * PART] = rows[k * PART : (k + 1) * PART, t * BLOCK : (t + 1) * BLOCK]
    for copy in copies:
        copy.wait()


def permute(mask, owner, own, matrix, coupling, after):
    return call(
        permute_kernel,
        [far(coupling.shape, BF16)] * 2 + [f32(SPLIT, NXY * PART, BLOCK), f32(NXY, 2 * OWN, BLOCK)],
        [HBM, HBM, VMEM, VMEM],
        [HBM] * 6,
        [
            pltpu.SMEM(mask.shape, jnp.int32),
            pltpu.VMEM(owner.shape, jnp.int32),
            pltpu.VMEM(own.shape, F32),
            pltpu.VMEM(matrix.shape, F32),
            pltpu.VMEM(coupling.shape, BF16),
            pltpu.VMEM(coupling.shape, BF16),
            DMA((5,)),
            DMA((2, coupling.shape[1] // TILE)),
        ],
        PERMUTE_MIB,
        mask, owner, own, matrix, coupling, after,
    )


def reorder_kernel(owner_in, mine, other, after, mine_out, other_out, token, owner, terms, sem):
    copy = pltpu.make_async_copy(owner_in, owner, sem)
    copy.start()
    span, count = BLOCK // (NZ * PART), NZ * PART
    token[...] = jnp.zeros(token.shape, F32)
    left = lax.broadcasted_iota(jnp.int32, (BLOCK, BLOCK), 0)
    right = lax.broadcasted_iota(jnp.int32, (BLOCK, BLOCK), 1)

    def by_block(k):
        return (k // PART) % span * count + k // (span * PART) * PART + k % PART

    gather = (left == by_block(right)).astype(BF16)
    scatter = (right == by_block(left)).astype(F32)
    for n, source in enumerate((mine, other)):
        base = source.shape[1] - NXY * PART
        for i in range(NXY // span):
            tile = source[:, base + 8 * i : base + 8 * (i + 1)].reshape(BLOCK, BLOCK)
            for m, term in enumerate(split3(tile)):
                moved = dot(gather, term).astype(BF16)
                for j in range(span):
                    row = (2 * m + n) * count
                    col = (span * i + j) * BLOCK
                    terms[row : row + count, col : col + BLOCK] = moved[j * count : (j + 1) * count]
    copy.wait()
    size = span * BLOCK
    for i in range(NXY // span):
        part = dot(terms[...], picks(owner, i, size))
        part = part[: 2 * count] + part[2 * count : 4 * count] + part[4 * count :]
        for n, out in enumerate((mine_out, other_out)):
            stack = jnp.concatenate(
                [part[n * count : (n + 1) * count, j * BLOCK : (j + 1) * BLOCK] for j in range(span)], axis=0
            )
            tile = jnp.dot(scatter, stack, precision=HIGHEST, preferred_element_type=F32)
            out[:, 8 * i : 8 * (i + 1)] = tile.reshape(NZ, 8, BLOCK)


def reorder(owner, mine, other, after):
    shape = (NZ, NXY * PART, BLOCK)
    return call(
        reorder_kernel,
        [f32(*shape)] * 2 + [f32(8, BLOCK)],
        [VMEM] * 3,
        [HBM, VMEM, VMEM, VMEM],
        [pltpu.VMEM(owner.shape, jnp.int32), pltpu.VMEM((6 * NZ * PART, NXY * BLOCK), BF16), DMA],
        PERMUTE_MIB,
        owner, mine, other, after,
    )


def local_kernel(core, place, sep, own, other, delta, after, out, rows, buf):
    first = core[0] == 0
    for t in range(NXY):
        mine, swapped = own[t], other[t, : 2 * OWN]
        low, high = jnp.where(first, mine, swapped), jnp.where(first, swapped, mine)
        rows[:, t * BLOCK : (t + 1) * BLOCK] = low + pltpu.roll(high, OWN, 0)
    left = split3(rows[...])
    total = sep[...]
    count = total.shape[0]
    for i, term in enumerate(split3(delta[...])):
        part = dot(join(left[: 3 - i]), term)
        for j in range(3 - i):
            total = total - part[j * count : (j + 1) * count]
    buf[...] = jnp.zeros(buf.shape, F32)
    buf[pl.ds(pl.multiple_of(place[0], 8), count), :] = total
    out[...] = buf[...].T


def case_group(total, z):
    group = total.shape[0] * SPLIT // NZ
    first = z // SPLIT * group
    return total[first : first + group]


def pack_sum_kernel(parts, packed, out):
    group = parts.shape[1] * SPLIT // NZ
    total = -jnp.sum(parts[...], axis=0)
    for z in range(NZ):
        out[z, :group] = case_group(total, z)
        out[z, group:] = packed[z % SPLIT]


def sum_rows_kernel(parts, local_t, after, out):
    total = local_t[...] - jnp.sum(parts[...], axis=0)
    for z in range(NZ):
        out[z] = case_group(total, z)


def sum_cases_kernel(parts, out):
    total = jnp.sum(parts[:, : out.shape[1]], axis=0)
    out[...] = jnp.broadcast_to(total[None], out.shape)


def sum_send_kernel(parts, matrix_rows, out, send):
    sum_cases_kernel(parts, out)
    send[:, : 2 * OWN] = matrix_rows[...]
    send[:, 2 * OWN :] = parts[:, out.shape[1] :]


def row_tile(rows, i):
    base = rows.shape[1] - NXY * PART
    return rows[:, base + 8 * i : base + 8 * (i + 1)].reshape(BLOCK, BLOCK)


def delta_kernel(core, rhs, mine, other, out):
    cases = rhs.shape[1]
    span = BLOCK // (NZ * PART)
    acc_mine = jnp.zeros((span * cases, BLOCK), F32)
    acc_other = jnp.zeros((span * cases, BLOCK), F32)
    for i in range(NXY // span):
        left = split3(rhs[span * i : span * (i + 1)].reshape(span * cases, BLOCK))
        acc_mine = acc_mine + rows_dot(left, row_tile(mine, i))
        acc_other = acc_other + rows_dot(left, row_tile(other, i))
    low = lax.broadcasted_iota(jnp.int32, (cases, BLOCK), 1) % 8 < PART

    def fold(acc):
        total = acc[:cases]
        for j in range(1, span):
            total = total + pltpu.roll(acc[j * cases : (j + 1) * cases], BLOCK - PART * j, 1)
        return jnp.where(low, total, 0.0)

    own, far_rows = fold(acc_mine), fold(acc_other)
    first = core[0] == 0
    total = jnp.where(first, own, far_rows) + pltpu.roll(jnp.where(first, far_rows, own), OWN, 1)
    half = cases // SPLIT
    tile = total[:half] + pltpu.roll(total[half:], PART, 1)
    out[...] = jnp.broadcast_to(tile[None], out.shape)


def rows_dot(left, rows):
    count = left[0].shape[0]
    total = jnp.zeros((count, rows.shape[0]), F32)
    for i, term in enumerate(split3(rows)):
        part = lax.dot_general(
            jnp.concatenate(left[: 3 - i], axis=0), term, (((1,), (1,)), ((), ())), preferred_element_type=F32
        )
        for j in range(3 - i):
            total = total + part[j * count : (j + 1) * count]
    return total


def unpacked(parts, cases_buf):
    half = parts.shape[1]
    low = lax.broadcasted_iota(jnp.int32, (half, BLOCK), 1) % (2 * PART) < PART
    for i in range(NZ // SPLIT):
        even, odd = parts[SPLIT * i], parts[SPLIT * i + 1]
        cases_buf[2 * half * i : 2 * half * i + half] = jnp.where(low, even, pltpu.roll(odd, PART, 1))
        cases_buf[2 * half * i + half : 2 * half * (i + 1)] = jnp.where(low, pltpu.roll(even, BLOCK - PART, 1), odd)
    return cases_buf[...].T


def spread_kernel(parts, out, cases_buf):
    out[...] = jnp.broadcast_to(unpacked(parts, cases_buf)[None], out.shape)


def own_rows(first, delta, count):
    return delta[pl.ds(pl.multiple_of(first[0], 8), count), :]


def middle_kernel(
    first, delta, cubic_row, columns, inverse, solved, matrix, load, mixed_out, contrib, sep_out,
    mixed, part_buf, mixed_sem, part_sems,
):
    sep_out[...] = own_rows(first, delta, sep_out.shape[0])
    cubic = jnp.broadcast_to(cubic_row[...], (8, cubic_row.shape[1])).T[:, :1]
    coupled = dot(columns[...], delta[...].astype(BF16))
    state = solved[...] - dot(inverse[...], coupled.astype(BF16))
    resid = load[...] - dot(matrix[...], state.astype(BF16)) - coupled
    resid = resid - cubic * state * state * state
    mixed[...] = state + dot(inverse[...], resid.astype(BF16))
    mixed_t = mixed[...].T.astype(BF16)
    count = part_sems.shape[0]
    size = columns.shape[1] // count
    copies = [pltpu.make_async_copy(mixed, mixed_out, mixed_sem)]
    copies[0].start()
    for i in range(count):
        part = dot(mixed_t, columns[:, i * size : (i + 1) * size])
        copies.append(send_tile(part, i, part_buf, contrib, part_sems))
    for copy in copies:
        copy.wait()


def end_kernel(first, delta, sep_in, columns, inverse, mixed, out, sep_out, state, out_sems):
    sep_out[...] = sep_in[...] + own_rows(first, delta, sep_out.shape[0])
    back = dot(columns[...], delta[...].astype(BF16)).astype(BF16)
    count = out_sems.shape[0]
    rows = state.shape[0] // count
    copies = []
    for i in range(count):
        part = pl.ds(i * rows, rows)
        state[part, :] = mixed[part, :] - dot(inverse[part, :], back)
        copy = pltpu.make_async_copy(state.at[part], out.at[part], out_sems.at[i])
        copy.start()
        copies.append(copy)
    for copy in copies:
        copy.wait()


def exchange(parts, axes):
    return lax.all_to_all(parts, axes, 0, 0, tiled=True)


def correction(contrib, core, packed, matrix_rows):
    cases = contrib.shape[1]
    group = cases * SPLIT // NZ
    parts = exchange(contrib, ("x", "y"))
    sent = f32(NZ, group + packed.shape[1], BLOCK)
    mine = exchange(call(pack_sum_kernel, sent, VMEM, [VMEM] * 2, [], 8, parts, packed), "z")
    rhs, send = call(
        sum_send_kernel,
        [f32(NXY, group, BLOCK), f32(NZ, 2 * OWN + packed.shape[1], BLOCK)],
        [VMEM] * 2,
        [VMEM] * 2,
        [],
        4,
        mine, matrix_rows,
    )
    other = lax.ppermute(send, "c", [(0, 1), (1, 0)])
    return solve(rhs, core, mine, other), mine, other


def second_correction(contrib, local_t, core, mine, other, owner):
    group = contrib.shape[1] * SPLIT // NZ
    parts = exchange(contrib, ("x", "y"))
    mine, other, token = reorder(owner, mine, other, local_t)
    parts = call(sum_rows_kernel, f32(NZ, group, BLOCK), VMEM, [VMEM] * 3, [], 8, parts, local_t, token)
    parts = exchange(parts, "z")
    rhs = call(sum_cases_kernel, f32(NXY, group, BLOCK), VMEM, [VMEM], [], 4, parts)
    return solve(rhs, core, mine, other)


def solve(rhs, core, mine, other):
    group = rhs.shape[1]
    cases = group * NZ // SPLIT
    rhs = exchange(rhs, ("x", "y"))
    delta = call(
        delta_kernel, f32(NZ, group // SPLIT, BLOCK), VMEM, [SMEM] + [VMEM] * 3, [], 8, core, rhs, mine, other
    )
    delta = exchange(delta, "z")
    delta = call(
        spread_kernel, f32(NXY, BLOCK, cases), VMEM, [VMEM], [pltpu.VMEM((cases, BLOCK), F32)], 4, delta
    )
    return exchange(delta, ("x", "y")).reshape(NXY * BLOCK, cases)


def on_device(
    leaf_matrix,
    leaf_inverse,
    coupling,
    cubic_coeff,
    leaf_load,
    sep_load,
    sep_matrix,
    sep_inverse,
    owner_map,
    block_mask,
):
    owned, cases = sep_load.shape
    width, sep_width = coupling.shape
    core = lax.axis_index("c").astype(jnp.int32)[None]
    place = (lax.axis_index("z") * owned).astype(jnp.int32)[None]
    first = (lax.axis_index(("x", "y", "z")) * owned).astype(jnp.int32)[None]
    owner = owner_map[None, :]
    solved, contrib = start(first, block_mask, leaf_inverse, coupling, leaf_load, owner, sep_load)
    columns, columns_again, packed, matrix_rows = permute(
        block_mask, owner, sep_inverse, sep_matrix, coupling, solved
    )

    delta, mine, other = correction(contrib, core, packed, matrix_rows)
    mixed, contrib, sep_rows = call(
        middle_kernel,
        [far((width, cases)), far((NXY, cases, BLOCK)), f32(owned, cases)],
        [HBM, HBM, VMEM],
        [SMEM] + [VMEM] * 7,
        [pltpu.VMEM((width, cases), F32), pltpu.VMEM((NXY, cases, BLOCK), F32), DMA, DMA((OUT_TILES,))],
        MIDDLE_MIB,
        first, delta, cubic_coeff[None, :], columns, leaf_inverse, solved, leaf_matrix, leaf_load,
    )
    local_t = call(
        local_kernel,
        f32(cases, BLOCK),
        VMEM,
        [SMEM] * 2 + [VMEM] * 4 + [HBM],
        [pltpu.VMEM((owned, sep_width), F32), pltpu.VMEM((BLOCK, cases), F32)],
        8,
        core, place, sep_load, matrix_rows, other, delta, contrib,
    )
    delta = second_correction(contrib, local_t, core, mine, other, owner)
    return call(
        end_kernel,
        [far((width, cases)), f32(owned, cases)],
        [HBM, VMEM],
        [SMEM] + [VMEM] * 5,
        [pltpu.VMEM((width, cases), F32), DMA((2,))],
        MIDDLE_MIB,
        first, delta, sep_rows, columns_again, leaf_inverse, mixed,
    )


def solution(mesh):
    grid = Mesh(mesh.devices.reshape(NX, NY, NZ, NC), ("x", "y", "z", "c"))
    leaf = ("x", "y", "z")
    in_specs = (
        P(leaf, None),
        P(leaf, None),
        P(leaf, None),
        P(leaf),
        P(leaf, "c"),
        P(leaf, "c"),
        P(leaf + ("c",), None),
        P(leaf + ("c",), None),
        P(),
        P(leaf, None),
    )
    out_specs = (P(leaf, "c"), P(leaf, "c"))
    return jax.shard_map(on_device, mesh=grid, in_specs=in_specs, out_specs=out_specs, check_vma=False)
```

```python
import jax
import jax.numpy as jnp
from jax import lax
from jax.experimental import pallas as pl
from jax.experimental.pallas import tpu as pltpu
from jax.sharding import Mesh, PartitionSpec as P

BLOCK = 128
NX, NY, NZ, NC = 4, 4, 16, 2
NXY = NX * NY
OWN = 4
SPLIT = 2
PART = OWN // SPLIT
TILE = 512
OUT_TILES = 4
START_MIB = 16
PERMUTE_MIB = 32
MIDDLE_MIB = 14
F32 = jnp.float32
BF16 = jnp.bfloat16
HIGHEST = lax.Precision.HIGHEST
MIB = 1024 * 1024
HBM = pl.BlockSpec(memory_space=pltpu.HBM)
SMEM = pl.BlockSpec(memory_space=pltpu.SMEM)
VMEM = pl.BlockSpec(memory_space=pltpu.VMEM)
DMA = pltpu.SemaphoreType.DMA


def dot(left, right):
    return jnp.dot(left, right, preferred_element_type=F32)


def f32(*shape):
    return jax.ShapeDtypeStruct(shape, F32)


def far(shape, dtype=F32):
    return pltpu.HBM(shape, dtype)


def call(kernel, out_shape, out_specs, in_specs, scratch, limit, *args):
    args = [pltpu.with_memory_space_constraint(x, pltpu.HBM) if spec is HBM else x for spec, x in zip(in_specs, args)]
    return pl.pallas_call(
        kernel,
        out_shape=out_shape,
        out_specs=out_specs,
        in_specs=in_specs,
        scratch_shapes=scratch,
        compiler_params=pltpu.CompilerParams(vmem_limit_bytes=limit * MIB),
    )(*args)


def fetch(sources, targets, sems):
    copies = [pltpu.make_async_copy(s, t, sems.at[i]) for i, (s, t) in enumerate(zip(sources, targets))]
    for copy in copies:
        copy.start()
    return copies


def send_tile(part, tile, scratch, contrib, sems):
    count = part.shape[1] // BLOCK
    first = tile * count
    for i in range(count):
        scratch[first + i] = part[:, i * BLOCK : (i + 1) * BLOCK]
    rows = pl.ds(first, count)
    copy = pltpu.make_async_copy(scratch.at[rows], contrib.at[rows], sems.at[tile])
    copy.start()
    return copy


def masked(mask, coupling):
    for i in range(coupling.shape[1] // BLOCK):
        cols = slice(i * BLOCK, (i + 1) * BLOCK)
        coupling[:, cols] = jnp.where(mask[0, i] != 0, coupling[:, cols], jnp.zeros((), BF16))


def picks(owner, tile, size):
    rows = lax.broadcasted_iota(jnp.int32, (owner.shape[1], size), 0)
    return (rows == owner[:, tile * size : (tile + 1) * size]).astype(BF16)


def split3(x):
    high = x.astype(BF16)
    rest = x - high.astype(F32)
    mid = rest.astype(BF16)
    return [high, mid, (rest - mid.astype(F32)).astype(BF16)]


def join(terms):
    return jnp.concatenate([x.astype(F32) for x in terms], axis=0).astype(BF16)


def start_kernel(
    first, core, place, mask_in, inverse_in, load_in, owner_in, sep_in, coupling_in, solved_out, contrib,
    mask, inverse, load, owner, sep, coupling, solved, part_buf, in_sems, out_sem, part_sems,
):
    waits = fetch(
        (mask_in, inverse_in, load_in, owner_in, sep_in, coupling_in),
        (mask, inverse, load, owner, sep, coupling),
        in_sems,
    )
    for wait in waits[1:3]:
        wait.wait()
    solved[...] = dot(inverse[...], load[...].astype(BF16))
    copies = [pltpu.make_async_copy(solved, solved_out, out_sem)]
    copies[0].start()
    mixed_t = solved[...].T.astype(BF16)
    for wait in waits[:1] + waits[3:]:
        wait.wait()
    own, sep_width = sep.shape[0], coupling.shape[1]
    loads_in = join(split3(sep[...]))
    size = sep_width // part_sems.shape[0]
    index = lax.broadcasted_iota(jnp.int32, (own, size), 0)
    target = jnp.zeros((own, size), jnp.int32)
    for j in range(own):
        target = jnp.where(index == j, owner[0, first[0] + j], target)
    for tile in range(part_sems.shape[0]):
        lanes = lax.broadcasted_iota(jnp.int32, (own, size), 1) + tile * size
        place = (lanes == target).astype(F32)
        loads = lax.dot_general(
            loads_in, join([place] * 3), (((0,), (0,)), ((), ())), preferred_element_type=F32
        )
        part = dot(mixed_t, coupling[:, tile * size : (tile + 1) * size])
        count = size // BLOCK
        kept = [
            jnp.where(mask[0, tile * count + i] != 0, part[:, i * BLOCK : (i + 1) * BLOCK], 0.0) for i in range(count)
        ]
        part = jnp.concatenate(kept, axis=1) - loads
        copies.append(send_tile(part, tile, part_buf, contrib, part_sems))
    for copy in copies:
        copy.wait()


def start(scalars, mask, inverse, coupling, load, owner, sep):
    cases = load.shape[1]
    return call(
        start_kernel,
        [far(load.shape), far((NXY, cases, BLOCK))],
        [HBM] * 2,
        [SMEM] * 3 + [HBM] * 6,
        [
            pltpu.SMEM(mask.shape, jnp.int32),
            pltpu.VMEM(inverse.shape, BF16),
            pltpu.VMEM(load.shape, F32),
            pltpu.SMEM(owner.shape, jnp.int32),
            pltpu.VMEM(sep.shape, F32),
            pltpu.VMEM(coupling.shape, BF16),
            pltpu.VMEM(load.shape, F32),
            pltpu.VMEM((NXY, cases, BLOCK), F32),
            DMA((6,)),
            DMA,
            DMA((OUT_TILES,)),
        ],
        START_MIB,
        *scalars, mask, inverse, load, owner, sep, coupling,
    )


def permute_kernel(
    mask_in, owner_in, own_in, matrix_in, coupling_in, after, columns_out, columns_again, packed, matrix_rows,
    mask, owner, own, matrix, coupling, columns, in_sems, out_sems,
):
    waits = fetch(
        (mask_in, owner_in, own_in, matrix_in, coupling_in), (mask, owner, own, matrix, coupling), in_sems
    )
    for wait in waits:
        wait.wait()
    matrix_rows[...] = jnp.zeros(matrix_rows.shape, F32)
    for t in range(NXY):
        matrix_rows[t, :OWN] = matrix[:, t * BLOCK : (t + 1) * BLOCK]
    masked(mask, coupling)
    terms = join(split3(own[...]))
    rows = jnp.zeros((3 * OWN, owner.shape[1]), F32)
    copies = []
    for tile in range(coupling.shape[1] // TILE):
        cols = pl.ds(tile * TILE, TILE)
        pick = picks(owner, tile, TILE)
        columns[:, cols] = dot(coupling[...], pick).astype(BF16)
        for i, out in enumerate((columns_out, columns_again)):
            copy = pltpu.make_async_copy(columns.at[:, cols], out.at[:, cols], out_sems.at[i, tile])
            copy.start()
            copies.append(copy)
        rows = rows + lax.dot_general(
            terms[:, tile * TILE : (tile + 1) * TILE], pick, (((1,), (1,)), ((), ())), preferred_element_type=F32
        )
    rows = rows[:OWN] + rows[OWN : 2 * OWN] + rows[2 * OWN :]
    for k in range(SPLIT):
        for t in range(NXY):
            packed[k, t * PART : (t + 1) * PART] = rows[k * PART : (k + 1) * PART, t * BLOCK : (t + 1) * BLOCK]
    for copy in copies:
        copy.wait()


def permute(mask, owner, own, matrix, coupling, after):
    return call(
        permute_kernel,
        [far(coupling.shape, BF16)] * 2 + [f32(SPLIT, NXY * PART, BLOCK), f32(NXY, 2 * OWN, BLOCK)],
        [HBM, HBM, VMEM, VMEM],
        [HBM] * 6,
        [
            pltpu.SMEM(mask.shape, jnp.int32),
            pltpu.VMEM(owner.shape, jnp.int32),
            pltpu.VMEM(own.shape, F32),
            pltpu.VMEM(matrix.shape, F32),
            pltpu.VMEM(coupling.shape, BF16),
            pltpu.VMEM(coupling.shape, BF16),
            DMA((5,)),
            DMA((2, coupling.shape[1] // TILE)),
        ],
        PERMUTE_MIB,
        mask, owner, own, matrix, coupling, after,
    )


def reorder_kernel(owner_in, mine, other, after, mine_out, other_out, token, owner, terms, sem):
    copy = pltpu.make_async_copy(owner_in, owner, sem)
    copy.start()
    span, count = BLOCK // (NZ * PART), NZ * PART
    token[...] = jnp.zeros(token.shape, F32)
    left = lax.broadcasted_iota(jnp.int32, (BLOCK, BLOCK), 0)
    right = lax.broadcasted_iota(jnp.int32, (BLOCK, BLOCK), 1)

    def by_block(k):
        return (k // PART) % span * count + k // (span * PART) * PART + k % PART

    gather = (left == by_block(right)).astype(BF16)
    scatter = (right == by_block(left)).astype(F32)
    for n, source in enumerate((mine, other)):
        base = source.shape[1] - NXY * PART
        for i in range(NXY // span):
            tile = source[:, base + 8 * i : base + 8 * (i + 1)].reshape(BLOCK, BLOCK)
            for m, term in enumerate(split3(tile)):
                moved = dot(gather, term).astype(BF16)
                for j in range(span):
                    row = (2 * m + n) * count
                    col = (span * i + j) * BLOCK
                    terms[row : row + count, col : col + BLOCK] = moved[j * count : (j + 1) * count]
    copy.wait()
    size = span * BLOCK
    for i in range(NXY // span):
        part = dot(terms[...], picks(owner, i, size))
        part = part[: 2 * count] + part[2 * count : 4 * count] + part[4 * count :]
        for n, out in enumerate((mine_out, other_out)):
            stack = jnp.concatenate(
                [part[n * count : (n + 1) * count, j * BLOCK : (j + 1) * BLOCK] for j in range(span)], axis=0
            )
            tile = jnp.dot(scatter, stack, precision=HIGHEST, preferred_element_type=F32)
            out[:, 8 * i : 8 * (i + 1)] = tile.reshape(NZ, 8, BLOCK)


def reorder(owner, mine, other, after):
    shape = (NZ, NXY * PART, BLOCK)
    return call(
        reorder_kernel,
        [f32(*shape)] * 2 + [f32(8, BLOCK)],
        [VMEM] * 3,
        [HBM, VMEM, VMEM, VMEM],
        [pltpu.VMEM(owner.shape, jnp.int32), pltpu.VMEM((6 * NZ * PART, NXY * BLOCK), BF16), DMA],
        PERMUTE_MIB,
        owner, mine, other, after,
    )


def local_kernel(core, place, sep, own, other, delta, after, out, rows, buf):
    first = core[0] == 0
    for t in range(NXY):
        mine, swapped = own[t], other[t, : 2 * OWN]
        low, high = jnp.where(first, mine, swapped), jnp.where(first, swapped, mine)
        rows[:, t * BLOCK : (t + 1) * BLOCK] = low + pltpu.roll(high, OWN, 0)
    left = split3(rows[...])
    total = sep[...]
    count = total.shape[0]
    for i, term in enumerate(split3(delta[...])):
        part = dot(join(left[: 3 - i]), term)
        for j in range(3 - i):
            total = total - part[j * count : (j + 1) * count]
    buf[...] = jnp.zeros(buf.shape, F32)
    buf[pl.ds(pl.multiple_of(place[0], 8), count), :] = total
    out[...] = buf[...].T


def case_group(total, z):
    group = total.shape[0] * SPLIT // NZ
    first = z // SPLIT * group
    return total[first : first + group]


def pack_sum_kernel(parts, packed, out):
    group = parts.shape[1] * SPLIT // NZ
    total = -jnp.sum(parts[...], axis=0)
    for z in range(NZ):
        out[z, :group] = case_group(total, z)
        out[z, group:] = packed[z % SPLIT]


def sum_rows_kernel(parts, local_t, after, out):
    total = local_t[...] - jnp.sum(parts[...], axis=0)
    for z in range(NZ):
        out[z] = case_group(total, z)


def sum_cases_kernel(parts, out):
    total = jnp.sum(parts[:, : out.shape[1]], axis=0)
    out[...] = jnp.broadcast_to(total[None], out.shape)


def sum_send_kernel(parts, matrix_rows, out, send):
    sum_cases_kernel(parts, out)
    send[:, : 2 * OWN] = matrix_rows[...]
    send[:, 2 * OWN :] = parts[:, out.shape[1] :]


def row_tile(rows, i):
    base = rows.shape[1] - NXY * PART
    return rows[:, base + 8 * i : base + 8 * (i + 1)].reshape(BLOCK, BLOCK)


def delta_kernel(core, rhs, mine, other, *after_and_out):
    out = after_and_out[-1]
    cases = rhs.shape[1]
    span = BLOCK // (NZ * PART)
    acc_mine = jnp.zeros((span * cases, BLOCK), F32)
    acc_other = jnp.zeros((span * cases, BLOCK), F32)
    for i in range(NXY // span):
        left = split3(rhs[span * i : span * (i + 1)].reshape(span * cases, BLOCK))
        acc_mine = acc_mine + rows_dot(left, row_tile(mine, i))
        acc_other = acc_other + rows_dot(left, row_tile(other, i))
    low = lax.broadcasted_iota(jnp.int32, (cases, BLOCK), 1) % 8 < PART

    def fold(acc):
        total = acc[:cases]
        for j in range(1, span):
            total = total + pltpu.roll(acc[j * cases : (j + 1) * cases], BLOCK - PART * j, 1)
        return jnp.where(low, total, 0.0)

    own, far_rows = fold(acc_mine), fold(acc_other)
    first = core[0] == 0
    total = jnp.where(first, own, far_rows) + pltpu.roll(jnp.where(first, far_rows, own), OWN, 1)
    half = cases // SPLIT
    tile = total[:half] + pltpu.roll(total[half:], PART, 1)
    out[...] = jnp.broadcast_to(tile[None], out.shape)


def rows_dot(left, rows):
    count = left[0].shape[0]
    total = jnp.zeros((count, rows.shape[0]), F32)
    for i, term in enumerate(split3(rows)):
        part = lax.dot_general(
            jnp.concatenate(left[: 3 - i], axis=0), term, (((1,), (1,)), ((), ())), preferred_element_type=F32
        )
        for j in range(3 - i):
            total = total + part[j * count : (j + 1) * count]
    return total


def unpacked(parts, cases_buf):
    half = parts.shape[1]
    low = lax.broadcasted_iota(jnp.int32, (half, BLOCK), 1) % (2 * PART) < PART
    for i in range(NZ // SPLIT):
        even, odd = parts[SPLIT * i], parts[SPLIT * i + 1]
        cases_buf[2 * half * i : 2 * half * i + half] = jnp.where(low, even, pltpu.roll(odd, PART, 1))
        cases_buf[2 * half * i + half : 2 * half * (i + 1)] = jnp.where(low, pltpu.roll(even, BLOCK - PART, 1), odd)
    return cases_buf[...].T


def spread_kernel(parts, out, cases_buf):
    out[...] = jnp.broadcast_to(unpacked(parts, cases_buf)[None], out.shape)


def own_rows(first, delta, count):
    return delta[pl.ds(pl.multiple_of(first[0], 8), count), :]


def middle_kernel(
    first, delta, cubic_row, columns, inverse, solved, matrix, load, mixed_out, contrib, sep_out,
    mixed, part_buf, mixed_sem, part_sems,
):
    sep_out[...] = own_rows(first, delta, sep_out.shape[0])
    cubic = jnp.broadcast_to(cubic_row[...], (8, cubic_row.shape[1])).T[:, :1]
    coupled = dot(columns[...], delta[...].astype(BF16))
    state = solved[...] - dot(inverse[...], coupled.astype(BF16))
    resid = load[...] - dot(matrix[...], state.astype(BF16)) - coupled
    resid = resid - cubic * state * state * state
    mixed[...] = state + dot(inverse[...], resid.astype(BF16))
    mixed_t = mixed[...].T.astype(BF16)
    count = part_sems.shape[0]
    size = columns.shape[1] // count
    copies = [pltpu.make_async_copy(mixed, mixed_out, mixed_sem)]
    copies[0].start()
    for i in range(count):
        part = dot(mixed_t, columns[:, i * size : (i + 1) * size])
        copies.append(send_tile(part, i, part_buf, contrib, part_sems))
    for copy in copies:
        copy.wait()


def end_kernel(first, delta, sep_in, columns, inverse, mixed, out, sep_out, state, out_sems):
    sep_out[...] = sep_in[...] + own_rows(first, delta, sep_out.shape[0])
    back = dot(columns[...], delta[...].astype(BF16)).astype(BF16)
    count = out_sems.shape[0]
    rows = state.shape[0] // count
    copies = []
    for i in range(count):
        part = pl.ds(i * rows, rows)
        state[part, :] = mixed[part, :] - dot(inverse[part, :], back)
        copy = pltpu.make_async_copy(state.at[part], out.at[part], out_sems.at[i])
        copy.start()
        copies.append(copy)
    for copy in copies:
        copy.wait()


def exchange(parts, axes):
    return lax.all_to_all(parts, axes, 0, 0, tiled=True)


def correction(contrib, core, packed, matrix_rows):
    cases = contrib.shape[1]
    group = cases * SPLIT // NZ
    parts = exchange(contrib, ("x", "y"))
    sent = f32(NZ, group + packed.shape[1], BLOCK)
    mine = exchange(call(pack_sum_kernel, sent, VMEM, [VMEM] * 2, [], 8, parts, packed), "z")
    rhs, send = call(
        sum_send_kernel,
        [f32(NXY, group, BLOCK), f32(NZ, 2 * OWN + packed.shape[1], BLOCK)],
        [VMEM] * 2,
        [VMEM] * 2,
        [],
        4,
        mine, matrix_rows,
    )
    other = lax.ppermute(send, "c", [(0, 1), (1, 0)])
    return solve(rhs, core, mine, other, between(rhs)), mine, other


def second_correction(contrib, local_t, core, mine, other, owner):
    group = contrib.shape[1] * SPLIT // NZ
    parts = exchange(contrib, ("x", "y"))
    mine, other, token = reorder(owner, mine, other, local_t)
    parts = call(sum_rows_kernel, f32(NZ, group, BLOCK), VMEM, [VMEM] * 3, [], 8, parts, local_t, token)
    parts = exchange(parts, "z")
    rhs = call(sum_cases_kernel, f32(NXY, group, BLOCK), VMEM, [VMEM], [], 4, parts)
    return solve(rhs, core, mine, other)


def between_kernel(rhs, out, sem):
    copy = pltpu.make_async_copy(rhs.at[0, :8], out, sem)
    copy.start()
    copy.wait()


def between(rhs):
    return pl.pallas_call(
        between_kernel,
        out_shape=far((8, BLOCK)),
        in_specs=[HBM],
        out_specs=HBM,
        scratch_shapes=[DMA],
        cost_estimate=pl.CostEstimate(flops=10**10, transcendentals=0, bytes_accessed=8192),
    )(pltpu.with_memory_space_constraint(rhs, pltpu.HBM))


def solve(rhs, core, mine, other, *after):
    group = rhs.shape[1]
    cases = group * NZ // SPLIT
    rhs = exchange(rhs, ("x", "y"))
    delta = call(
        delta_kernel,
        f32(NZ, group // SPLIT, BLOCK),
        VMEM,
        [SMEM] + [VMEM] * 3 + [HBM] * len(after),
        [],
        8,
        core, rhs, mine, other, *after,
    )
    delta = exchange(delta, "z")
    delta = call(
        spread_kernel, f32(NXY, BLOCK, cases), VMEM, [VMEM], [pltpu.VMEM((cases, BLOCK), F32)], 4, delta
    )
    return exchange(delta, ("x", "y")).reshape(NXY * BLOCK, cases)


def on_device(
    leaf_matrix,
    leaf_inverse,
    coupling,
    cubic_coeff,
    leaf_load,
    sep_load,
    sep_matrix,
    sep_inverse,
    owner_map,
    block_mask,
):
    owned, cases = sep_load.shape
    width, sep_width = coupling.shape
    core = lax.axis_index("c").astype(jnp.int32)[None]
    place = (lax.axis_index("z") * owned).astype(jnp.int32)[None]
    first = (lax.axis_index(("x", "y", "z")) * owned).astype(jnp.int32)[None]
    owner = owner_map[None, :]
    solved, contrib = start((first, core, place), block_mask, leaf_inverse, coupling, leaf_load, owner, sep_load)
    columns, columns_again, packed, matrix_rows = permute(
        block_mask, owner, sep_inverse, sep_matrix, coupling, solved
    )

    delta, mine, other = correction(contrib, core, packed, matrix_rows)
    mixed, contrib, sep_rows = call(
        middle_kernel,
        [far((width, cases)), far((NXY, cases, BLOCK)), f32(owned, cases)],
        [HBM, HBM, VMEM],
        [SMEM] + [VMEM] * 7,
        [pltpu.VMEM((width, cases), F32), pltpu.VMEM((NXY, cases, BLOCK), F32), DMA, DMA((OUT_TILES,))],
        MIDDLE_MIB,
        first, delta, cubic_coeff[None, :], columns, leaf_inverse, solved, leaf_matrix, leaf_load,
    )
    local_t = call(
        local_kernel,
        f32(cases, BLOCK),
        VMEM,
        [SMEM] * 2 + [VMEM] * 4 + [HBM],
        [pltpu.VMEM((owned, sep_width), F32), pltpu.VMEM((BLOCK, cases), F32)],
        8,
        core, place, sep_load, matrix_rows, other, delta, contrib,
    )
    delta = second_correction(contrib, local_t, core, mine, other, owner)
    return call(
        end_kernel,
        [far((width, cases)), f32(owned, cases)],
        [HBM, VMEM],
        [SMEM] + [VMEM] * 5,
        [pltpu.VMEM((width, cases), F32), DMA((2,))],
        MIDDLE_MIB,
        first, delta, sep_rows, columns_again, leaf_inverse, mixed,
    )


def solution(mesh):
    grid = Mesh(mesh.devices.reshape(NX, NY, NZ, NC), ("x", "y", "z", "c"))
    leaf = ("x", "y", "z")
    in_specs = (
        P(leaf, None),
        P(leaf, None),
        P(leaf, None),
        P(leaf),
        P(leaf, "c"),
        P(leaf, "c"),
        P(leaf + ("c",), None),
        P(leaf + ("c",), None),
        P(),
        P(leaf, None),
    )
    out_specs = (P(leaf, "c"), P(leaf, "c"))
    return jax.shard_map(on_device, mesh=grid, in_specs=in_specs, out_specs=out_specs, check_vma=False)
```

```python
import jax
import jax.numpy as jnp
from jax import lax
from jax.experimental import pallas as pl
from jax.experimental.pallas import tpu as pltpu
from jax.sharding import Mesh, PartitionSpec as P

BLOCK = 128
NX, NY, NZ, NC = 4, 4, 16, 2
NXY = NX * NY
OWN = 4
SPLIT = 2
PART = OWN // SPLIT
TILE = 512
OUT_TILES = 4
START_MIB = 16
PERMUTE_MIB = 32
MIDDLE_MIB = 14
F32 = jnp.float32
BF16 = jnp.bfloat16
HIGHEST = lax.Precision.HIGHEST
MIB = 1024 * 1024
HBM = pl.BlockSpec(memory_space=pltpu.HBM)
SMEM = pl.BlockSpec(memory_space=pltpu.SMEM)
VMEM = pl.BlockSpec(memory_space=pltpu.VMEM)
DMA = pltpu.SemaphoreType.DMA


def dot(left, right):
    return jnp.dot(left, right, preferred_element_type=F32)


def f32(*shape):
    return jax.ShapeDtypeStruct(shape, F32)


def far(shape, dtype=F32):
    return pltpu.HBM(shape, dtype)


def call(kernel, out_shape, out_specs, in_specs, scratch, limit, *args):
    args = [pltpu.with_memory_space_constraint(x, pltpu.HBM) if spec is HBM else x for spec, x in zip(in_specs, args)]
    return pl.pallas_call(
        kernel,
        out_shape=out_shape,
        out_specs=out_specs,
        in_specs=in_specs,
        scratch_shapes=scratch,
        compiler_params=pltpu.CompilerParams(vmem_limit_bytes=limit * MIB),
    )(*args)


def fetch(sources, targets, sems):
    copies = [pltpu.make_async_copy(s, t, sems.at[i]) for i, (s, t) in enumerate(zip(sources, targets))]
    for copy in copies:
        copy.start()
    return copies


def send_tile(part, tile, scratch, contrib, sems):
    count = part.shape[1] // BLOCK
    first = tile * count
    for i in range(count):
        scratch[first + i] = part[:, i * BLOCK : (i + 1) * BLOCK]
    rows = pl.ds(first, count)
    copy = pltpu.make_async_copy(scratch.at[rows], contrib.at[rows], sems.at[tile])
    copy.start()
    return copy


def masked(mask, coupling):
    for i in range(coupling.shape[1] // BLOCK):
        cols = slice(i * BLOCK, (i + 1) * BLOCK)
        coupling[:, cols] = jnp.where(mask[0, i] != 0, coupling[:, cols], jnp.zeros((), BF16))


def picks(owner, tile, size):
    rows = lax.broadcasted_iota(jnp.int32, (owner.shape[1], size), 0)
    return (rows == owner[:, tile * size : (tile + 1) * size]).astype(BF16)


def split3(x):
    high = x.astype(BF16)
    rest = x - high.astype(F32)
    mid = rest.astype(BF16)
    return [high, mid, (rest - mid.astype(F32)).astype(BF16)]


def join(terms):
    return jnp.concatenate([x.astype(F32) for x in terms], axis=0).astype(BF16)


def targets(first, owner, own, size):
    index = lax.broadcasted_iota(jnp.int32, (own, size), 0)
    target = jnp.zeros((own, size), jnp.int32)
    for j in range(own):
        target = jnp.where(index == j, owner[0, first[0] + j], target)
    return target


def part_tile(mixed_t, coupling, mask, terms, target, tile):
    own, size = target.shape
    lanes = lax.broadcasted_iota(jnp.int32, (own, size), 1) + tile * size
    place = (lanes == target).astype(F32)
    loads = lax.dot_general(terms, join([place] * 3), (((0,), (0,)), ((), ())), preferred_element_type=F32)
    part = dot(mixed_t, coupling[:, tile * size : (tile + 1) * size])
    count = size // BLOCK
    kept = [
        jnp.where(mask[0, tile * count + i] != 0, part[:, i * BLOCK : (i + 1) * BLOCK], 0.0) for i in range(count)
    ]
    return jnp.concatenate(kept, axis=1) - loads


def start_kernel(
    first, core, mask_in, inverse_in, load_in, owner_in, sep_in, coupling_in, solved_out, contrib,
    mask, inverse, load, owner, sep, coupling, solved, part_buf, in_sems, out_sem, part_sems,
):
    waits = fetch(
        (mask_in, inverse_in, load_in, owner_in, sep_in, coupling_in),
        (mask, inverse, load, owner, sep, coupling),
        in_sems,
    )
    for wait in waits[1:3]:
        wait.wait()
    solved[...] = dot(inverse[...], load[...].astype(BF16))
    copies = [pltpu.make_async_copy(solved, solved_out, out_sem)]
    copies[0].start()
    mixed_t = solved[...].T.astype(BF16)
    for wait in waits[:1] + waits[3:]:
        wait.wait()
    terms = join(split3(sep[...]))
    target = targets(first, owner, sep.shape[0], coupling.shape[1] // part_sems.shape[0])
    for tile in range(part_sems.shape[0]):
        part = part_tile(mixed_t, coupling, mask, terms, target, tile)
        copies.append(send_tile(part, tile, part_buf, contrib, part_sems))
    for copy in copies:
        copy.wait()


def start(scalars, mask, inverse, coupling, load, owner, sep):
    cases = load.shape[1]
    return call(
        start_kernel,
        [far(load.shape), far((NXY, cases, BLOCK))],
        [HBM] * 2,
        [SMEM] * 2 + [HBM] * 6,
        [
            pltpu.SMEM(mask.shape, jnp.int32),
            pltpu.VMEM(inverse.shape, BF16),
            pltpu.VMEM(load.shape, F32),
            pltpu.SMEM(owner.shape, jnp.int32),
            pltpu.VMEM(sep.shape, F32),
            pltpu.VMEM(coupling.shape, BF16),
            pltpu.VMEM(load.shape, F32),
            pltpu.VMEM((NXY, cases, BLOCK), F32),
            DMA((6,)),
            DMA,
            DMA((OUT_TILES,)),
        ],
        START_MIB,
        *scalars, mask, inverse, load, owner, sep, coupling,
    )


def permute_kernel(
    mask_in, owner_in, own_in, matrix_in, coupling_in, after, columns_out, columns_again, packed, matrix_rows,
    mask, owner, own, matrix, coupling, columns, in_sems, out_sems,
):
    waits = fetch(
        (mask_in, owner_in, own_in, matrix_in, coupling_in), (mask, owner, own, matrix, coupling), in_sems
    )
    for wait in waits:
        wait.wait()
    matrix_rows[...] = jnp.zeros(matrix_rows.shape, F32)
    for t in range(NXY):
        matrix_rows[t, :OWN] = matrix[:, t * BLOCK : (t + 1) * BLOCK]
    masked(mask, coupling)
    terms = join(split3(own[...]))
    rows = jnp.zeros((3 * OWN, owner.shape[1]), F32)
    copies = []
    for tile in range(coupling.shape[1] // TILE):
        cols = pl.ds(tile * TILE, TILE)
        pick = picks(owner, tile, TILE)
        columns[:, cols] = dot(coupling[...], pick).astype(BF16)
        for i, out in enumerate((columns_out, columns_again)):
            copy = pltpu.make_async_copy(columns.at[:, cols], out.at[:, cols], out_sems.at[i, tile])
            copy.start()
            copies.append(copy)
        rows = rows + lax.dot_general(
            terms[:, tile * TILE : (tile + 1) * TILE], pick, (((1,), (1,)), ((), ())), preferred_element_type=F32
        )
    rows = rows[:OWN] + rows[OWN : 2 * OWN] + rows[2 * OWN :]
    for k in range(SPLIT):
        for t in range(NXY):
            packed[k, t * PART : (t + 1) * PART] = rows[k * PART : (k + 1) * PART, t * BLOCK : (t + 1) * BLOCK]
    for copy in copies:
        copy.wait()


def permute(mask, owner, own, matrix, coupling, after):
    return call(
        permute_kernel,
        [far(coupling.shape, BF16)] * 2 + [f32(SPLIT, NXY * PART, BLOCK), f32(NXY, 2 * OWN, BLOCK)],
        [HBM, HBM, VMEM, VMEM],
        [HBM] * 6,
        [
            pltpu.SMEM(mask.shape, jnp.int32),
            pltpu.VMEM(owner.shape, jnp.int32),
            pltpu.VMEM(own.shape, F32),
            pltpu.VMEM(matrix.shape, F32),
            pltpu.VMEM(coupling.shape, BF16),
            pltpu.VMEM(coupling.shape, BF16),
            DMA((5,)),
            DMA((2, coupling.shape[1] // TILE)),
        ],
        PERMUTE_MIB,
        mask, owner, own, matrix, coupling, after,
    )


def local_rows(core, sep, own, other, delta, rows):
    first = core[0] == 0
    for t in range(NXY):
        mine, swapped = own[t], other[t, : 2 * OWN]
        low, high = jnp.where(first, mine, swapped), jnp.where(first, swapped, mine)
        rows[:, t * BLOCK : (t + 1) * BLOCK] = low + pltpu.roll(high, OWN, 0)
    left = split3(rows[...])
    total = sep[...]
    count = total.shape[0]
    for i, term in enumerate(split3(delta[...])):
        part = dot(join(left[: 3 - i]), term)
        for j in range(3 - i):
            total = total - part[j * count : (j + 1) * count]
    return total


def case_group(total, z):
    group = total.shape[0] * SPLIT // NZ
    first = z // SPLIT * group
    return total[first : first + group]


def pack_sum_kernel(parts, packed, out):
    group = parts.shape[1] * SPLIT // NZ
    total = -jnp.sum(parts[...], axis=0)
    for z in range(NZ):
        out[z, :group] = case_group(total, z)
        out[z, group:] = packed[z % SPLIT]


def sum_rows_kernel(parts, out):
    total = -jnp.sum(parts[...], axis=0)
    for z in range(NZ):
        out[z] = case_group(total, z)


def sum_cases_kernel(parts, out):
    total = jnp.sum(parts[:, : out.shape[1]], axis=0)
    out[...] = jnp.broadcast_to(total[None], out.shape)


def sum_send_kernel(parts, matrix_rows, out, send):
    sum_cases_kernel(parts, out)
    send[:, : 2 * OWN] = matrix_rows[...]
    send[:, 2 * OWN :] = parts[:, out.shape[1] :]


def row_tile(rows, i):
    base = rows.shape[1] - NXY * PART
    return rows[:, base + 8 * i : base + 8 * (i + 1)].reshape(BLOCK, BLOCK)


def delta_kernel(core, rhs, mine, other, *after_and_out):
    out = after_and_out[-1]
    cases = rhs.shape[1]
    span = BLOCK // (NZ * PART)
    acc_mine = jnp.zeros((span * cases, BLOCK), F32)
    acc_other = jnp.zeros((span * cases, BLOCK), F32)
    for i in range(NXY // span):
        left = split3(rhs[span * i : span * (i + 1)].reshape(span * cases, BLOCK))
        acc_mine = acc_mine + rows_dot(left, row_tile(mine, i))
        acc_other = acc_other + rows_dot(left, row_tile(other, i))
    low = lax.broadcasted_iota(jnp.int32, (cases, BLOCK), 1) % 8 < PART

    def fold(acc):
        total = acc[:cases]
        for j in range(1, span):
            total = total + pltpu.roll(acc[j * cases : (j + 1) * cases], BLOCK - PART * j, 1)
        return jnp.where(low, total, 0.0)

    own, far_rows = fold(acc_mine), fold(acc_other)
    first = core[0] == 0
    total = jnp.where(first, own, far_rows) + pltpu.roll(jnp.where(first, far_rows, own), OWN, 1)
    half = cases // SPLIT
    tile = total[:half] + pltpu.roll(total[half:], PART, 1)
    out[...] = jnp.broadcast_to(tile[None], out.shape)


def rows_dot(left, rows):
    count = left[0].shape[0]
    total = jnp.zeros((count, rows.shape[0]), F32)
    for i, term in enumerate(split3(rows)):
        part = lax.dot_general(
            jnp.concatenate(left[: 3 - i], axis=0), term, (((1,), (1,)), ((), ())), preferred_element_type=F32
        )
        for j in range(3 - i):
            total = total + part[j * count : (j + 1) * count]
    return total


def unpacked(parts, cases_buf):
    half = parts.shape[1]
    low = lax.broadcasted_iota(jnp.int32, (half, BLOCK), 1) % (2 * PART) < PART
    for i in range(NZ // SPLIT):
        even, odd = parts[SPLIT * i], parts[SPLIT * i + 1]
        cases_buf[2 * half * i : 2 * half * i + half] = jnp.where(low, even, pltpu.roll(odd, PART, 1))
        cases_buf[2 * half * i + half : 2 * half * (i + 1)] = jnp.where(low, pltpu.roll(even, BLOCK - PART, 1), odd)
    return cases_buf[...].T


def spread_kernel(parts, out, cases_buf):
    out[...] = jnp.broadcast_to(unpacked(parts, cases_buf)[None], out.shape)


def own_rows(first, delta, count):
    return delta[pl.ds(pl.multiple_of(first[0], 8), count), :]


def middle_kernel(
    first, core, mask_in, owner_in, coupling_in, delta, cubic_row, columns, inverse, solved, matrix, load,
    sep, matrix_rows, other, mixed_out, contrib, sep_out, mask, owner, coupling, mixed, rows, in_sems, mixed_sem,
):
    waits = fetch((mask_in, owner_in, coupling_in), (mask, owner, coupling), in_sems)
    sep_out[...] = own_rows(first, delta, sep_out.shape[0])
    cubic = jnp.broadcast_to(cubic_row[...], (8, cubic_row.shape[1])).T[:, :1]
    coupled = dot(columns[...], delta[...].astype(BF16))
    terms = join(split3(local_rows(core, sep, matrix_rows, other, delta, rows)))
    state = solved[...] - dot(inverse[...], coupled.astype(BF16))
    resid = load[...] - dot(matrix[...], state.astype(BF16)) - coupled
    resid = resid - cubic * state * state * state
    mixed[...] = state + dot(inverse[...], resid.astype(BF16))
    copy = pltpu.make_async_copy(mixed, mixed_out, mixed_sem)
    copy.start()
    mixed_t = mixed[...].T.astype(BF16)
    for wait in waits:
        wait.wait()
    size = coupling.shape[1] // OUT_TILES
    target = targets(first, owner, sep.shape[0], size)
    for tile in range(OUT_TILES):
        part = part_tile(mixed_t, coupling, mask, terms, target, tile)
        for i in range(size // BLOCK):
            contrib[tile * (size // BLOCK) + i] = part[:, i * BLOCK : (i + 1) * BLOCK]
    copy.wait()


def end_kernel(first, delta, sep_in, columns, inverse, mixed, out, sep_out, state, out_sems):
    sep_out[...] = sep_in[...] + own_rows(first, delta, sep_out.shape[0])
    back = dot(columns[...], delta[...].astype(BF16)).astype(BF16)
    count = out_sems.shape[0]
    rows = state.shape[0] // count
    copies = []
    for i in range(count):
        part = pl.ds(i * rows, rows)
        state[part, :] = mixed[part, :] - dot(inverse[part, :], back)
        copy = pltpu.make_async_copy(state.at[part], out.at[part], out_sems.at[i])
        copy.start()
        copies.append(copy)
    for copy in copies:
        copy.wait()


def exchange(parts, axes):
    return lax.all_to_all(parts, axes, 0, 0, tiled=True)


def correction(contrib, core, packed, matrix_rows):
    cases = contrib.shape[1]
    group = cases * SPLIT // NZ
    parts = exchange(contrib, ("x", "y"))
    sent = f32(NZ, group + packed.shape[1], BLOCK)
    mine = exchange(call(pack_sum_kernel, sent, VMEM, [VMEM] * 2, [], 8, parts, packed), "z")
    rhs, send = call(
        sum_send_kernel,
        [f32(NXY, group, BLOCK), f32(NZ, 2 * OWN + packed.shape[1], BLOCK)],
        [VMEM] * 2,
        [VMEM] * 2,
        [],
        4,
        mine, matrix_rows,
    )
    other = lax.ppermute(send, "c", [(0, 1), (1, 0)])
    return solve(rhs, core, mine, other, between(rhs)), mine, other


def second_correction(contrib, core, mine, other):
    group = contrib.shape[1] * SPLIT // NZ
    parts = exchange(contrib, ("x", "y"))
    parts = call(sum_rows_kernel, f32(NZ, group, BLOCK), VMEM, [VMEM], [], 8, parts)
    parts = exchange(parts, "z")
    rhs = call(sum_cases_kernel, f32(NXY, group, BLOCK), VMEM, [VMEM], [], 4, parts)
    return solve(rhs, core, mine, other)


def between_kernel(rhs, out, sem):
    copy = pltpu.make_async_copy(rhs.at[0, :8], out, sem)
    copy.start()
    copy.wait()


def between(rhs):
    return pl.pallas_call(
        between_kernel,
        out_shape=far((8, BLOCK)),
        in_specs=[HBM],
        out_specs=HBM,
        scratch_shapes=[DMA],
        cost_estimate=pl.CostEstimate(flops=10**10, transcendentals=0, bytes_accessed=8192),
    )(pltpu.with_memory_space_constraint(rhs, pltpu.HBM))


def solve(rhs, core, mine, other, *after):
    group = rhs.shape[1]
    cases = group * NZ // SPLIT
    rhs = exchange(rhs, ("x", "y"))
    delta = call(
        delta_kernel,
        f32(NZ, group // SPLIT, BLOCK),
        VMEM,
        [SMEM] + [VMEM] * 3 + [HBM] * len(after),
        [],
        8,
        core, rhs, mine, other, *after,
    )
    delta = exchange(delta, "z")
    delta = call(
        spread_kernel, f32(NXY, BLOCK, cases), VMEM, [VMEM], [pltpu.VMEM((cases, BLOCK), F32)], 4, delta
    )
    return exchange(delta, ("x", "y")).reshape(NXY * BLOCK, cases)


def on_device(
    leaf_matrix,
    leaf_inverse,
    coupling,
    cubic_coeff,
    leaf_load,
    sep_load,
    sep_matrix,
    sep_inverse,
    owner_map,
    block_mask,
):
    owned, cases = sep_load.shape
    width, sep_width = coupling.shape
    core = lax.axis_index("c").astype(jnp.int32)[None]
    first = (lax.axis_index(("x", "y", "z")) * owned).astype(jnp.int32)[None]
    owner = owner_map[None, :]
    solved, contrib = start((first, core), block_mask, leaf_inverse, coupling, leaf_load, owner, sep_load)
    columns, columns_again, packed, matrix_rows = permute(
        block_mask, owner, sep_inverse, sep_matrix, coupling, solved
    )

    delta, mine, other = correction(contrib, core, packed, matrix_rows)
    mixed, contrib, sep_rows = call(
        middle_kernel,
        [far((width, cases)), f32(NXY, cases, BLOCK), f32(owned, cases)],
        [HBM, VMEM, VMEM],
        [SMEM] * 2 + [HBM] * 3 + [VMEM] * 10,
        [
            pltpu.SMEM(block_mask.shape, jnp.int32),
            pltpu.SMEM(owner.shape, jnp.int32),
            pltpu.VMEM(coupling.shape, BF16),
            pltpu.VMEM((width, cases), F32),
            pltpu.VMEM((owned, sep_width), F32),
            DMA((3,)),
            DMA,
        ],
        MIDDLE_MIB,
        first, core, block_mask, owner, coupling, delta, cubic_coeff[None, :], columns, leaf_inverse, solved, leaf_matrix,
        leaf_load, sep_load, matrix_rows, other,
    )
    delta = second_correction(contrib, core, mine, other)
    return call(
        end_kernel,
        [far((width, cases)), f32(owned, cases)],
        [HBM, VMEM],
        [SMEM] + [VMEM] * 5,
        [pltpu.VMEM((width, cases), F32), DMA((2,))],
        MIDDLE_MIB,
        first, delta, sep_rows, columns_again, leaf_inverse, mixed,
    )


def solution(mesh):
    grid = Mesh(mesh.devices.reshape(NX, NY, NZ, NC), ("x", "y", "z", "c"))
    leaf = ("x", "y", "z")
    in_specs = (
        P(leaf, None),
        P(leaf, None),
        P(leaf, None),
        P(leaf),
        P(leaf, "c"),
        P(leaf, "c"),
        P(leaf + ("c",), None),
        P(leaf + ("c",), None),
        P(),
        P(leaf, None),
    )
    out_specs = (P(leaf, "c"), P(leaf, "c"))
    return jax.shard_map(on_device, mesh=grid, in_specs=in_specs, out_specs=out_specs, check_vma=False)
```

```python
import jax
import jax.numpy as jnp
from jax import lax
from jax.experimental import pallas as pl
from jax.experimental.pallas import tpu as pltpu
from jax.sharding import Mesh, PartitionSpec as P

BLOCK = 128
NX, NY, NZ, NC = 4, 4, 16, 2
NXY = NX * NY
OWN = 4
SPLIT = 2
PART = OWN // SPLIT
TILE = 512
OUT_TILES = 4
START_MIB = 16
PERMUTE_MIB = 32
MIDDLE_MIB = 14
F32 = jnp.float32
BF16 = jnp.bfloat16
HIGHEST = lax.Precision.HIGHEST
MIB = 1024 * 1024
HBM = pl.BlockSpec(memory_space=pltpu.HBM)
SMEM = pl.BlockSpec(memory_space=pltpu.SMEM)
VMEM = pl.BlockSpec(memory_space=pltpu.VMEM)
DMA = pltpu.SemaphoreType.DMA


def dot(left, right):
    return jnp.dot(left, right, preferred_element_type=F32)


def f32(*shape):
    return jax.ShapeDtypeStruct(shape, F32)


def far(shape, dtype=F32):
    return pltpu.HBM(shape, dtype)


def call(kernel, out_shape, out_specs, in_specs, scratch, limit, *args):
    args = [pltpu.with_memory_space_constraint(x, pltpu.HBM) if spec is HBM else x for spec, x in zip(in_specs, args)]
    return pl.pallas_call(
        kernel,
        out_shape=out_shape,
        out_specs=out_specs,
        in_specs=in_specs,
        scratch_shapes=scratch,
        compiler_params=pltpu.CompilerParams(vmem_limit_bytes=limit * MIB),
    )(*args)


def fetch(sources, targets, sems):
    copies = [pltpu.make_async_copy(s, t, sems.at[i]) for i, (s, t) in enumerate(zip(sources, targets))]
    for copy in copies:
        copy.start()
    return copies


def send_tile(part, tile, scratch, contrib, sems):
    count = part.shape[1] // BLOCK
    first = tile * count
    for i in range(count):
        scratch[first + i] = part[:, i * BLOCK : (i + 1) * BLOCK]
    rows = pl.ds(first, count)
    copy = pltpu.make_async_copy(scratch.at[rows], contrib.at[rows], sems.at[tile])
    copy.start()
    return copy


def masked(mask, coupling):
    for i in range(coupling.shape[1] // BLOCK):
        cols = slice(i * BLOCK, (i + 1) * BLOCK)
        coupling[:, cols] = jnp.where(mask[0, i] != 0, coupling[:, cols], jnp.zeros((), BF16))


def picks(owner, tile, size):
    rows = lax.broadcasted_iota(jnp.int32, (owner.shape[1], size), 0)
    return (rows == owner[:, tile * size : (tile + 1) * size]).astype(BF16)


def split3(x):
    high = x.astype(BF16)
    rest = x - high.astype(F32)
    mid = rest.astype(BF16)
    return [high, mid, (rest - mid.astype(F32)).astype(BF16)]


def join(terms):
    return jnp.concatenate([x.astype(F32) for x in terms], axis=0).astype(BF16)


def targets(first, owner, own, size):
    index = lax.broadcasted_iota(jnp.int32, (own, size), 0)
    target = jnp.zeros((own, size), jnp.int32)
    for j in range(own):
        target = jnp.where(index == j, owner[0, first[0] + j], target)
    return target


def part_tile(mixed_t, coupling, mask, terms, target, tile):
    own, size = target.shape
    lanes = lax.broadcasted_iota(jnp.int32, (own, size), 1) + tile * size
    place = (lanes == target).astype(F32)
    loads = lax.dot_general(terms, join([place] * 3), (((0,), (0,)), ((), ())), preferred_element_type=F32)
    part = dot(mixed_t, coupling[:, tile * size : (tile + 1) * size])
    count = size // BLOCK
    kept = [
        jnp.where(mask[0, tile * count + i] != 0, part[:, i * BLOCK : (i + 1) * BLOCK], 0.0) for i in range(count)
    ]
    return jnp.concatenate(kept, axis=1) - loads


def start_kernel(
    first, core, mask_in, inverse_in, load_in, owner_in, sep_in, coupling_in, solved_out, contrib,
    mask, inverse, load, owner, sep, coupling, solved, part_buf, in_sems, out_sem, part_sems,
):
    waits = fetch(
        (mask_in, inverse_in, load_in, owner_in, sep_in, coupling_in),
        (mask, inverse, load, owner, sep, coupling),
        in_sems,
    )
    for wait in waits[1:3]:
        wait.wait()
    solved[...] = dot(inverse[...], load[...].astype(BF16))
    copies = [pltpu.make_async_copy(solved, solved_out, out_sem)]
    copies[0].start()
    mixed_t = solved[...].T.astype(BF16)
    for wait in waits[:1] + waits[3:]:
        wait.wait()
    terms = join(split3(sep[...]))
    target = targets(first, owner, sep.shape[0], coupling.shape[1] // part_sems.shape[0])
    for tile in range(part_sems.shape[0]):
        part = part_tile(mixed_t, coupling, mask, terms, target, tile)
        copies.append(send_tile(part, tile, part_buf, contrib, part_sems))
    for copy in copies:
        copy.wait()


def start(scalars, mask, inverse, coupling, load, owner, sep):
    cases = load.shape[1]
    return call(
        start_kernel,
        [far(load.shape), far((NXY, cases, BLOCK))],
        [HBM] * 2,
        [SMEM] * 2 + [HBM] * 6,
        [
            pltpu.SMEM(mask.shape, jnp.int32),
            pltpu.VMEM(inverse.shape, BF16),
            pltpu.VMEM(load.shape, F32),
            pltpu.SMEM(owner.shape, jnp.int32),
            pltpu.VMEM(sep.shape, F32),
            pltpu.VMEM(coupling.shape, BF16),
            pltpu.VMEM(load.shape, F32),
            pltpu.VMEM((NXY, cases, BLOCK), F32),
            DMA((6,)),
            DMA,
            DMA((OUT_TILES,)),
        ],
        START_MIB,
        *scalars, mask, inverse, load, owner, sep, coupling,
    )


def permute_kernel(
    mask_in, owner_in, own_in, matrix_in, coupling_in, after, columns_out, columns_again, packed, matrix_rows,
    mask, owner, own, matrix, coupling, columns, in_sems, out_sems,
):
    waits = fetch(
        (mask_in, owner_in, own_in, matrix_in, coupling_in), (mask, owner, own, matrix, coupling), in_sems
    )
    for wait in waits:
        wait.wait()
    matrix_rows[...] = jnp.zeros(matrix_rows.shape, F32)
    for t in range(NXY):
        matrix_rows[t, :OWN] = matrix[:, t * BLOCK : (t + 1) * BLOCK]
    masked(mask, coupling)
    terms = join(split3(own[...]))
    rows = jnp.zeros((3 * OWN, owner.shape[1]), F32)
    copies = []
    for tile in range(coupling.shape[1] // TILE):
        cols = pl.ds(tile * TILE, TILE)
        pick = picks(owner, tile, TILE)
        columns[:, cols] = dot(coupling[...], pick).astype(BF16)
        for i, out in enumerate((columns_out, columns_again)):
            copy = pltpu.make_async_copy(columns.at[:, cols], out.at[:, cols], out_sems.at[i, tile])
            copy.start()
            copies.append(copy)
        rows = rows + lax.dot_general(
            terms[:, tile * TILE : (tile + 1) * TILE], pick, (((1,), (1,)), ((), ())), preferred_element_type=F32
        )
    rows = rows[:OWN] + rows[OWN : 2 * OWN] + rows[2 * OWN :]
    for k in range(SPLIT):
        for t in range(NXY):
            packed[k, t * PART : (t + 1) * PART] = rows[k * PART : (k + 1) * PART, t * BLOCK : (t + 1) * BLOCK]
    for copy in copies:
        copy.wait()


def permute(mask, owner, own, matrix, coupling, after):
    return call(
        permute_kernel,
        [far(coupling.shape, BF16)] * 2 + [f32(SPLIT, NXY * PART, BLOCK), f32(NXY, 2 * OWN, BLOCK)],
        [HBM, HBM, VMEM, VMEM],
        [HBM] * 6,
        [
            pltpu.SMEM(mask.shape, jnp.int32),
            pltpu.VMEM(owner.shape, jnp.int32),
            pltpu.VMEM(own.shape, F32),
            pltpu.VMEM(matrix.shape, F32),
            pltpu.VMEM(coupling.shape, BF16),
            pltpu.VMEM(coupling.shape, BF16),
            DMA((5,)),
            DMA((2, coupling.shape[1] // TILE)),
        ],
        PERMUTE_MIB,
        mask, owner, own, matrix, coupling, after,
    )


def local_rows(core, sep, own, other, delta, rows):
    first = core[0] == 0
    for t in range(NXY):
        mine, swapped = own[t], other[t, : 2 * OWN]
        low, high = jnp.where(first, mine, swapped), jnp.where(first, swapped, mine)
        rows[:, t * BLOCK : (t + 1) * BLOCK] = low + pltpu.roll(high, OWN, 0)
    left = split3(rows[...])
    total = sep[...]
    count = total.shape[0]
    for i, term in enumerate(split3(delta[...])):
        part = dot(join(left[: 3 - i]), term)
        for j in range(3 - i):
            total = total - part[j * count : (j + 1) * count]
    return total


def case_group(total, z):
    group = total.shape[0] * SPLIT // NZ
    first = z // SPLIT * group
    return total[first : first + group]


def pack_sum_kernel(parts, packed, out):
    group = parts.shape[1] * SPLIT // NZ
    total = -jnp.sum(parts[...], axis=0)
    for z in range(NZ):
        out[z, :group] = case_group(total, z)
        out[z, group:] = packed[z % SPLIT]


def sum_rows_kernel(parts, out):
    total = -jnp.sum(parts[...], axis=0)
    for z in range(NZ):
        out[z] = case_group(total, z)


def sum_cases_kernel(parts, out):
    total = jnp.sum(parts[:, : out.shape[1]], axis=0)
    out[...] = jnp.broadcast_to(total[None], out.shape)


def sum_send_kernel(parts, matrix_rows, out, send):
    sum_cases_kernel(parts, out)
    send[:, : 2 * OWN] = matrix_rows[...]
    send[:, 2 * OWN :] = parts[:, out.shape[1] :]


def row_tile(rows, i):
    base = rows.shape[1] - NXY * PART
    return rows[:, base + 8 * i : base + 8 * (i + 1)].reshape(BLOCK, BLOCK)


def delta_kernel(core, rhs, mine, other, *after_and_out):
    out = after_and_out[-1]
    cases = rhs.shape[1]
    span = BLOCK // (NZ * PART)
    acc_mine = jnp.zeros((span * cases, BLOCK), F32)
    acc_other = jnp.zeros((span * cases, BLOCK), F32)
    for i in range(NXY // span):
        left = split3(rhs[span * i : span * (i + 1)].reshape(span * cases, BLOCK))
        acc_mine = acc_mine + rows_dot(left, row_tile(mine, i))
        acc_other = acc_other + rows_dot(left, row_tile(other, i))
    low = lax.broadcasted_iota(jnp.int32, (cases, BLOCK), 1) % 8 < PART

    def fold(acc):
        total = acc[:cases]
        for j in range(1, span):
            total = total + pltpu.roll(acc[j * cases : (j + 1) * cases], BLOCK - PART * j, 1)
        return jnp.where(low, total, 0.0)

    own, far_rows = fold(acc_mine), fold(acc_other)
    first = core[0] == 0
    total = jnp.where(first, own, far_rows) + pltpu.roll(jnp.where(first, far_rows, own), OWN, 1)
    half = cases // SPLIT
    tile = total[:half] + pltpu.roll(total[half:], PART, 1)
    out[...] = jnp.broadcast_to(tile[None], out.shape)


def rows_dot(left, rows):
    count = left[0].shape[0]
    total = jnp.zeros((count, rows.shape[0]), F32)
    for i, term in enumerate(split3(rows)):
        part = lax.dot_general(
            jnp.concatenate(left[: 3 - i], axis=0), term, (((1,), (1,)), ((), ())), preferred_element_type=F32
        )
        for j in range(3 - i):
            total = total + part[j * count : (j + 1) * count]
    return total


def unpacked(parts, cases_buf):
    half = parts.shape[1]
    low = lax.broadcasted_iota(jnp.int32, (half, BLOCK), 1) % (2 * PART) < PART
    for i in range(NZ // SPLIT):
        even, odd = parts[SPLIT * i], parts[SPLIT * i + 1]
        cases_buf[2 * half * i : 2 * half * i + half] = jnp.where(low, even, pltpu.roll(odd, PART, 1))
        cases_buf[2 * half * i + half : 2 * half * (i + 1)] = jnp.where(low, pltpu.roll(even, BLOCK - PART, 1), odd)
    return cases_buf[...].T


def spread_kernel(parts, out, cases_buf):
    out[...] = jnp.broadcast_to(unpacked(parts, cases_buf)[None], out.shape)


def own_rows(first, delta, count):
    return delta[pl.ds(pl.multiple_of(first[0], 8), count), :]


def middle_kernel(
    first, core, mask_in, owner_in, coupling_in, delta, cubic_row, columns, inverse, solved, matrix, load,
    sep, matrix_rows, other, mixed_out, contrib, sep_out, mask, owner, coupling, mixed, rows, in_sems, mixed_sem,
):
    waits = fetch((mask_in, owner_in, coupling_in), (mask, owner, coupling), in_sems)
    sep_out[...] = own_rows(first, delta, sep_out.shape[0])
    cubic = jnp.broadcast_to(cubic_row[...], (8, cubic_row.shape[1])).T[:, :1]
    coupled = dot(columns[...], delta[...].astype(BF16))
    terms = join(split3(local_rows(core, sep, matrix_rows, other, delta, rows)))
    state = solved[...] - dot(inverse[...], coupled.astype(BF16))
    resid = load[...] - dot(matrix[...], state.astype(BF16)) - coupled
    resid = resid - cubic * state * state * state
    mixed[...] = state + dot(inverse[...], resid.astype(BF16))
    copy = pltpu.make_async_copy(mixed, mixed_out, mixed_sem)
    copy.start()
    mixed_t = mixed[...].T.astype(BF16)
    for wait in waits:
        wait.wait()
    size = coupling.shape[1] // OUT_TILES
    target = targets(first, owner, sep.shape[0], size)
    for tile in range(OUT_TILES):
        part = part_tile(mixed_t, coupling, mask, terms, target, tile)
        for i in range(size // BLOCK):
            contrib[tile * (size // BLOCK) + i] = part[:, i * BLOCK : (i + 1) * BLOCK]
    copy.wait()


def end_kernel(first, delta, sep_in, columns, inverse, mixed, out, sep_out, state, out_sems):
    sep_out[...] = sep_in[...] + own_rows(first, delta, sep_out.shape[0])
    back = dot(columns[...], delta[...].astype(BF16)).astype(BF16)
    count = out_sems.shape[0]
    rows = state.shape[0] // count
    copies = []
    for i in range(count):
        part = pl.ds(i * rows, rows)
        state[part, :] = mixed[part, :] - dot(inverse[part, :], back)
        copy = pltpu.make_async_copy(state.at[part], out.at[part], out_sems.at[i])
        copy.start()
        copies.append(copy)
    for copy in copies:
        copy.wait()


def exchange(parts, axes):
    return lax.all_to_all(parts, axes, 0, 0, tiled=True)


def correction(contrib, core, packed, matrix_rows):
    cases = contrib.shape[1]
    group = cases * SPLIT // NZ
    parts = exchange(contrib, ("x", "y"))
    sent = f32(NZ, group + packed.shape[1], BLOCK)
    mine = exchange(call(pack_sum_kernel, sent, VMEM, [VMEM] * 2, [], 8, parts, packed), "z")
    rhs, send = call(
        sum_send_kernel,
        [f32(NXY, group, BLOCK), f32(NZ, 2 * OWN + packed.shape[1], BLOCK)],
        [VMEM] * 2,
        [VMEM] * 2,
        [],
        4,
        mine, matrix_rows,
    )
    other = lax.ppermute(send, "c", [(0, 1), (1, 0)])
    return solve(rhs, core, mine, other, between(rhs)), mine, other


def second_correction(contrib, core, mine, other):
    group = contrib.shape[1] * SPLIT // NZ
    parts = exchange(contrib, ("x", "y"))
    parts = call(sum_rows_kernel, f32(NZ, group, BLOCK), VMEM, [VMEM], [], 8, parts)
    parts = exchange(parts, "z")
    rhs = call(sum_cases_kernel, f32(NXY, group, BLOCK), VMEM, [VMEM], [], 4, parts)
    return solve(rhs, core, mine, other)


def between_kernel(rhs, out):
    pass


def between(rhs):
    return pl.pallas_call(
        between_kernel,
        out_shape=far((8, BLOCK)),
        in_specs=[HBM],
        out_specs=HBM,
        cost_estimate=pl.CostEstimate(flops=10**10, transcendentals=0, bytes_accessed=8192),
    )(pltpu.with_memory_space_constraint(rhs, pltpu.HBM))


def solve(rhs, core, mine, other, *after):
    group = rhs.shape[1]
    cases = group * NZ // SPLIT
    rhs = exchange(rhs, ("x", "y"))
    delta = call(
        delta_kernel,
        f32(NZ, group // SPLIT, BLOCK),
        VMEM,
        [SMEM] + [VMEM] * 3 + [HBM] * len(after),
        [],
        8,
        core, rhs, mine, other, *after,
    )
    delta = exchange(delta, "z")
    delta = call(
        spread_kernel, f32(NXY, BLOCK, cases), VMEM, [VMEM], [pltpu.VMEM((cases, BLOCK), F32)], 4, delta
    )
    return exchange(delta, ("x", "y")).reshape(NXY * BLOCK, cases)


def on_device(
    leaf_matrix,
    leaf_inverse,
    coupling,
    cubic_coeff,
    leaf_load,
    sep_load,
    sep_matrix,
    sep_inverse,
    owner_map,
    block_mask,
):
    owned, cases = sep_load.shape
    width, sep_width = coupling.shape
    core = lax.axis_index("c").astype(jnp.int32)[None]
    first = (lax.axis_index(("x", "y", "z")) * owned).astype(jnp.int32)[None]
    owner = owner_map[None, :]
    solved, contrib = start((first, core), block_mask, leaf_inverse, coupling, leaf_load, owner, sep_load)
    columns, columns_again, packed, matrix_rows = permute(
        block_mask, owner, sep_inverse, sep_matrix, coupling, solved
    )

    delta, mine, other = correction(contrib, core, packed, matrix_rows)
    mixed, contrib, sep_rows = call(
        middle_kernel,
        [far((width, cases)), f32(NXY, cases, BLOCK), f32(owned, cases)],
        [HBM, VMEM, VMEM],
        [SMEM] * 2 + [HBM] * 3 + [VMEM] * 10,
        [
            pltpu.SMEM(block_mask.shape, jnp.int32),
            pltpu.SMEM(owner.shape, jnp.int32),
            pltpu.VMEM(coupling.shape, BF16),
            pltpu.VMEM((width, cases), F32),
            pltpu.VMEM((owned, sep_width), F32),
            DMA((3,)),
            DMA,
        ],
        MIDDLE_MIB,
        first, core, block_mask, owner, coupling, delta, cubic_coeff[None, :], columns, leaf_inverse, solved, leaf_matrix,
        leaf_load, sep_load, matrix_rows, other,
    )
    delta = second_correction(contrib, core, mine, other)
    return call(
        end_kernel,
        [far((width, cases)), f32(owned, cases)],
        [HBM, VMEM],
        [SMEM] + [VMEM] * 5,
        [pltpu.VMEM((width, cases), F32), DMA((2,))],
        MIDDLE_MIB,
        first, delta, sep_rows, columns_again, leaf_inverse, mixed,
    )


def solution(mesh):
    grid = Mesh(mesh.devices.reshape(NX, NY, NZ, NC), ("x", "y", "z", "c"))
    leaf = ("x", "y", "z")
    in_specs = (
        P(leaf, None),
        P(leaf, None),
        P(leaf, None),
        P(leaf),
        P(leaf, "c"),
        P(leaf, "c"),
        P(leaf + ("c",), None),
        P(leaf + ("c",), None),
        P(),
        P(leaf, None),
    )
    out_specs = (P(leaf, "c"), P(leaf, "c"))
    return jax.shard_map(on_device, mesh=grid, in_specs=in_specs, out_specs=out_specs, check_vma=False)
```
